32 devices in a mesh: wave: 8 (over z, x), grp: 4 (over y, core).
Axes of the slice: x: 2, y: 2, z: 4, core: 2. Of those that a mesh axis runs over, the one named last changes fastest.
Arguments:
- spectrum: float32 [1152, 16384], P('grp', 'wave'), may hold values from 0.2 to 2
- edge_vectors: float32 [2, 8, 16384], P(None, None, 'wave'), may hold values from -0.06 to 0.06
- neighbours: int32 [8, 16384], P(None, 'wave'), may hold values from 0 to 2303, as said below
- halo_lists: int32 [2, 8, 128], P(None, 'wave'), may hold values from 0 to 2047, as said below
- group_speed: float32 [32], P('grp'), may hold values from 0.5 to 1.5
- input_coef: float32 [32], P('grp'), may hold values from 0.3 to 1
- dissipation: float32 [32], P('grp'), may hold values from 0.05 to 0.5
- friction: float32 [16384], P('wave'), may hold values from 0.1 to 1
- wind_dir: float32 [16384], P('wave'), may hold values from -3.140625 to 3.140625
- drift_kernel: float32 [40, 1152], P(None, 'grp'), may hold values from -0.1875 to 0.1875
- block_tile: int32 [256], P('wave'), may hold values from 0 to 31, as said below
- block_weights: float32 [256, 64, 512], P('wave'), may hold values from -0.75 to 0.75
Outputs:
- updated: float32 [1152, 16384], P('grp', 'wave')
- drift: float32 [32, 40, 512], P('wave', None, 'grp')
The draws below stay inside these ranges and needn't reach their ends.
Inputs may be any that keep to these rules, and one draw needn't show every extreme that they name: `neighbours`: entry [n, j] indexes the extended points of point j's partition: below 2048 one of its own points, then the 128 points from the previous partition, then the 128 from the next; a padding entry is the point's own index j % 2048. `halo_lists`: local indices of a partition's own points; repeats are allowed. `block_tile`: block b lies on partition b // 32; tile t belongs to partition t // 4. The 32 blocks of one partition feed the tiles of any one partition at most 8 times, and in every draw one partition receives exactly 8 blocks from every partition.
All inputs are finite; a program needn't handle non-finite values.
Results may differ from the reference program's by a relative error of at most 0.000071.
Values sent between devices are 32-bit elements; how exact they have to be, the bound alone decides.
No kernel may reach another device: no remote copies, remote signals or barrier semaphores. Data moves between devices by JAX's collectives and lax.ppermute only.
A program may use at most 128 MiB of HBM per device.

```python
import math
import jax
import jax.numpy as jnp
from jax import lax

ND = 36
NF = 32
NB = 8
HALO = 128
BPD = 32
BLK = 64
TC = 512
TPW = 4
PARTS_SIZE = 8
P_DEV = 2048
NPTS = 16384
NBLK = 256
NTILE = 32
NBINS = 1152
NZ2 = 40
CAP = 8


def draw_neighbours(key, part):
    pick_key, pad_key = jax.random.split(key)
    own_index = jnp.arange(NPTS, dtype=jnp.int32) % P_DEV
    picked = jax.random.randint(pick_key, (NB, NPTS), 0, P_DEV + 2 * HALO, dtype=jnp.int32)
    padded = jax.random.randint(pad_key, (NB, NPTS), 0, 4, dtype=jnp.int32) == 0
    result = jnp.where(padded, own_index[None, :], picked)
    result = result.at[0, 0].set(0).at[1, 0].set(P_DEV + 2 * HALO - 1)
    return result.astype(jnp.int32)


def draw_halo_lists(key, part):
    listed = jax.random.randint(key, (2, PARTS_SIZE, HALO), 0, P_DEV, dtype=jnp.int32)
    listed = listed.at[:, :, 0].set(P_DEV - 1).at[:, :, 1].set(0)
    return listed.astype(jnp.int32)


def draw_block_tile(key, part):
    hot_key, rest_key = jax.random.split(key)
    hottest = jax.random.randint(hot_key, (), 0, PARTS_SIZE, dtype=jnp.int32)

    def source_blocks(source_key):
        slot_key, order_key, offset_key = jax.random.split(source_key, 3)
        slot_ids = jax.random.permutation(slot_key, (PARTS_SIZE - 1) * CAP)[:BPD - CAP]
        others = (slot_ids // CAP).astype(jnp.int32)
        others = others + (others >= hottest).astype(jnp.int32)
        targets = jnp.concatenate([jnp.zeros((CAP,), jnp.int32) + hottest, others])
        targets = targets[jax.random.permutation(order_key, BPD)]
        offsets = jax.random.randint(offset_key, (BPD,), 0, TPW, dtype=jnp.int32)
        return targets * TPW + offsets
    source_keys = jax.random.split(rest_key, PARTS_SIZE)
    return jax.vmap(source_blocks)(source_keys).reshape(NBLK).astype(jnp.int32)


def block_levels(stream_key, extent, cuts, smallest, top_value):
    level = 1.0
    for position, blocks in cuts:
        draws = jax.random.uniform(jax.random.fold_in(jax.random.fold_in(stream_key, 6), position), (blocks,), jnp.float32, smallest / len(cuts), top_value / len(cuts))
        level = level * jnp.repeat(jnp.exp(draws), extent[position] // blocks).reshape((-1,) + (1,) * (len(extent) - 1 - position))
    return level


def centred(rng, shape, width, most, pieces=(), kind=jnp.bfloat16):
    drawn = jax.random.normal(rng, shape, jnp.float32) * width
    if len(pieces) > 0:
        drawn = block_levels(rng, shape, pieces, -0.22, 0.18) * drawn
    return jnp.clip(drawn, min=-most, max=most).astype(kind)


def setup_inputs(seed: int = 0) -> dict:
    key_of = jax.random.split(jax.random.key(seed), 13)
    return {
        "spectrum": jnp.clip(0.2 + 1.8 * jax.random.uniform(key_of[0], (NBINS, NPTS), jnp.float32) ** block_levels(key_of[0], (NBINS, NPTS), ((0, 4), (1, 8)), -0.2, 0.2), 0.2, 2.0),
        "edge_vectors": jnp.clip(jax.random.uniform(key_of[1], (2, NB, NPTS), jnp.float32, -0.06, 0.06) * block_levels(key_of[1], (2, NB, NPTS), ((2, 8),), -0.4, 0.0), -0.06, 0.06),
        "neighbours": draw_neighbours(jax.random.fold_in(key_of[12], 71), 0),
        "halo_lists": draw_halo_lists(jax.random.fold_in(key_of[12], 71), 0),
        "group_speed": jnp.clip(jnp.exp(math.log(1.5) - 1.0986123 * jax.random.uniform(key_of[4], (NF,), jnp.float32) ** block_levels(key_of[4], (NF,), ((0, 4),), -0.2, 0.2)), 0.5, 1.5),
        "input_coef": jnp.clip(jnp.exp(math.log(1.0) - 1.2039728 * jax.random.uniform(key_of[5], (NF,), jnp.float32) ** block_levels(key_of[5], (NF,), ((0, 4),), -0.2, 0.2)), 0.3, 1.0),
        "dissipation": jnp.clip(jnp.exp(math.log(0.5) - 2.3025851 * jax.random.uniform(key_of[6], (NF,), jnp.float32) ** block_levels(key_of[6], (NF,), ((0, 4),), -0.2, 0.2)), 0.05, 0.5),
        "friction": jnp.clip(jnp.exp(math.log(1.0) - 2.3025851 * jax.random.uniform(key_of[7], (NPTS,), jnp.float32) ** block_levels(key_of[7], (NPTS,), ((0, 8),), -0.2, 0.2)), 0.1, 1.0),
        "wind_dir": jnp.clip(jax.random.uniform(key_of[8], (NPTS,), jnp.float32, -3.140625, 3.140625), -3.140625, 3.140625),
        "drift_kernel": centred(key_of[9], (NZ2, NBINS), NBINS ** -0.5, 0.1875, ((1, 4),), jnp.float32),
        "block_tile": draw_block_tile(jax.random.fold_in(key_of[12], 71), 0),
        "block_weights": centred(key_of[11], (NBLK, BLK, TC), BLK ** -0.5, 0.75, ((0, 8),), jnp.float32),
    }


def global_neighbours(neighbours, halo_lists):
    point = jnp.arange(NPTS, dtype=jnp.int32)
    partition = (point // P_DEV)[None, :]
    local_index = neighbours
    own_point = partition * P_DEV + local_index
    prev_part = partition - 1
    prev_slot = jnp.clip(local_index - P_DEV, 0, HALO - 1)
    prev_point = halo_lists[0][jnp.clip(prev_part, 0, PARTS_SIZE - 1), prev_slot] + prev_part * P_DEV
    next_part = partition + 1
    next_slot = jnp.clip(local_index - P_DEV - HALO, 0, HALO - 1)
    next_point = halo_lists[1][jnp.clip(next_part, 0, PARTS_SIZE - 1), next_slot] + next_part * P_DEV
    is_prev = (local_index >= P_DEV) & (local_index < P_DEV + HALO)
    is_next = local_index >= P_DEV + HALO
    index = jnp.where(is_next, next_point, jnp.where(is_prev, prev_point, own_point))
    usable = jnp.logical_not((is_prev & (partition == 0)) | (is_next & (partition == PARTS_SIZE - 1)))
    return jnp.clip(index, 0, NPTS - 1).astype(jnp.int32), usable


def reference(spectrum, edge_vectors, neighbours, halo_lists, group_speed, input_coef, dissipation, friction, wind_dir, drift_kernel, block_tile, block_weights):
    index, usable = global_neighbours(neighbours, halo_lists)
    theta = jnp.arange(ND, dtype=jnp.float32) * (2.0 * math.pi / ND)
    cos_dir = jnp.cos(theta)
    sin_dir = jnp.sin(theta)
    wind_cos = jnp.cos(wind_dir)
    wind_sin = jnp.sin(wind_dir)

    def one_frequency(inputs):
        energy, speed, coef, loss = inputs
        along_x = (speed * cos_dir)[:, None]
        along_y = (speed * sin_dir)[:, None]
        inflow_sum = jnp.zeros(energy.shape, jnp.float32)
        for column in range(NB):
            projected = along_x * edge_vectors[0, column][None, :] + along_y * edge_vectors[1, column][None, :]
            inflow = jnp.maximum(-projected, 0.0)
            upwind = jnp.where(usable[column][None, :], jnp.take(energy, index[column], axis=1), 0.0)
            inflow_sum = inflow_sum + inflow * (upwind - energy)
        advected = energy + inflow_sum
        facing = jnp.maximum(cos_dir[:, None] * wind_cos[None, :] + sin_dir[:, None] * wind_sin[None, :], 0.0)
        growth = coef * friction[None, :] * facing - loss
        return advected * jnp.exp(growth)

    updated = lax.map(one_frequency, (spectrum.reshape(NF, ND, NPTS), group_speed, input_coef, dissipation))
    updated = updated.reshape(NBINS, NPTS)
    stokes = jnp.dot(drift_kernel, updated, precision=lax.Precision.HIGHEST, preferred_element_type=jnp.float32)
    per_block = stokes.reshape(NZ2, NBLK, BLK)
    terms = jnp.einsum("zbj,bjc->bzc", per_block, block_weights, precision=lax.Precision.HIGHEST)
    drift = jnp.zeros((NTILE, NZ2, TC), jnp.float32).at[block_tile].add(terms)
    return updated, drift
```

```python
import functools
import math

import jax
import jax.numpy as jnp
import ml_dtypes
import numpy as np
from jax import lax
from jax.experimental import pallas as pl
from jax.experimental.pallas import tpu as pltpu
from jax.sharding import PartitionSpec as P

ND = 36
TPW = 4
LANES = 128
PAIR = 2 * ND
BF = jnp.bfloat16
F32 = jnp.float32
VMEM = pl.BlockSpec(memory_space=pltpu.VMEM)
SMEM = pl.BlockSpec(memory_space=pltpu.SMEM)
ANY = pl.BlockSpec(memory_space=pl.ANY)


def params(mib):
    return pltpu.CompilerParams(vmem_limit_bytes=mib << 20)


def split2(x):
    high = x.astype(BF)
    return high, (x - high.astype(F32)).astype(BF)


def dot(a, b):
    return jnp.dot(a, b, preferred_element_type=F32)


def direction_constants(slots):
    theta = np.arange(ND) * (2.0 * math.pi / ND)
    cosine, sine = np.cos(theta), np.sin(theta)
    table = np.zeros((2, slots, slots, LANES), np.float32)
    for slot in range(slots):
        for half in range(2):
            table[0, slot, slot, half * ND : (half + 1) * ND] = -cosine
            table[1, slot, slot, half * ND : (half + 1) * ND] = -sine
    table = table.reshape(2 * slots, slots * LANES)
    high = table.astype(ml_dtypes.bfloat16)
    low = (table - high.astype(np.float32)).astype(ml_dtypes.bfloat16)
    rows = np.stack([np.tile(cosine, 2), np.tile(sine, 2)]).astype(np.float32)
    facing = np.broadcast_to(rows[:, :, None], (2, PAIR, LANES))
    return np.concatenate([high, low, high], 0), np.ascontiguousarray(facing)


def halo_kernel(lists_ref, spec_ref, next_ref, prev_ref):
    points = spec_ref.shape[1]
    step = 256
    totals = [None, None]
    for start in range(0, points, step):
        high, rest = spec_ref[:, start : start + step], None
        first = high.astype(BF)
        rest = high - first.astype(F32)
        second = rest.astype(BF)
        third = (rest - second.astype(F32)).astype(BF)
        ids = lax.broadcasted_iota(jnp.int32, (step, LANES), 0) + start
        for side in range(2):
            chosen = jnp.where(ids == lists_ref[side], 1.0, 0.0).astype(BF)
            part = dot(first, chosen) + dot(second, chosen) + dot(third, chosen)
            totals[side] = part if totals[side] is None else totals[side] + part
    next_ref[...] = totals[0]
    prev_ref[...] = totals[1]


def pick_halo(spectrum, lists):
    bins = spectrum.shape[0]
    shape = jax.ShapeDtypeStruct((bins, lists.shape[-1]), F32)
    return pl.pallas_call(
        halo_kernel,
        in_specs=[VMEM, VMEM],
        out_specs=[VMEM, VMEM],
        out_shape=[shape, shape],
        compiler_params=params(40),
    )(lists, spectrum)


def advance_kernel(
    index_ref,
    speed_ref,
    coef_ref,
    loss_ref,
    spec_ref,
    prev_ref,
    next_ref,
    edge_ref,
    air_ref,
    weight_ref,
    facing_ref,
    kernel_ref,
    updated_ref,
    stokes_ref,
    table,
    inflow,
    gathered,
    result,
    sems,
    *,
    unroll,
):
    bins, points = spec_ref.shape
    groups = bins // PAIR
    slots = edge_ref.shape[0] // 2
    halo = prev_ref.shape[1]
    blocks = points // LANES
    filler = jnp.zeros((LANES - PAIR, LANES), F32)

    def place(x, group, block):
        rows = pl.ds(block * (LANES * groups) + group, LANES, stride=groups)
        table[rows, :] = jnp.concatenate([x, filler], 0).T

    @pl.loop(0, blocks)
    def _(block):
        columns = pl.ds(pl.multiple_of(block * LANES, LANES), LANES)
        for group in range(groups):
            place(spec_ref[group * PAIR : (group + 1) * PAIR, columns], group, block)

    for group in range(groups):
        rows = slice(group * PAIR, (group + 1) * PAIR)
        place(prev_ref[rows, :], group, blocks)
        place(next_ref[rows, :], group, blocks + halo // LANES)

    kernel_high, kernel_low = split2(kernel_ref[...])
    kernel_both = jnp.concatenate([kernel_high, kernel_low], 0)
    depth = kernel_ref.shape[0]

    def copy_out(block):
        columns = pl.ds(pl.multiple_of(block * LANES, LANES), LANES)
        return pltpu.make_async_copy(
            result.at[block], updated_ref.at[:, columns], sems.at[block]
        )

    @pl.loop(0, blocks)
    def _(block):
        base = pl.multiple_of(block * LANES, LANES)
        columns = pl.ds(base, LANES)
        edge_high, edge_low = split2(edge_ref[:, columns])
        left = jnp.concatenate([edge_high, edge_high, edge_low], 0)
        weights = lax.dot_general(
            left, weight_ref[...], (((0,), (0,)), ((), ())), preferred_element_type=F32
        )
        for slot in range(slots):
            inflow[slot, :LANES, :] = jnp.maximum(weights[:, slot * LANES : (slot + 1) * LANES], 0.0)

        @pl.loop(0, LANES // unroll)
        def _(chunk):
            first = pl.multiple_of(chunk * unroll, unroll)
            for u in range(unroll):
                point = first + u
                picks = index_ref.at[pl.ds((base + point) * slots, slots)]
                own = table[pl.ds((base + point) * groups, groups), :]
                terms = []
                for slot in range(slots):
                    upwind = table[pl.ds(picks[slot], groups), :]
                    factor = inflow[slot, pl.ds(point, groups, stride=0), :]
                    terms.append(factor * (upwind - own))
                while len(terms) > 1:
                    terms = [a + b for a, b in zip(terms[::2], terms[1::2])]
                gathered[pl.ds(point * groups, groups), :] = terms[0]

        cos_wind = air_ref[0:1, columns]
        sin_wind = air_ref[1:2, columns]
        friction = air_ref[2:3, columns]
        facing = jnp.maximum(facing_ref[0] * cos_wind + facing_ref[1] * sin_wind, 0.0)
        pushed = facing * friction
        lower = lax.broadcasted_iota(jnp.int32, (PAIR, LANES), 0) < ND

        def per_bin(ref, group):
            return jnp.where(lower, ref[2 * group], ref[2 * group + 1])

        for group in range(groups):
            rows = slice(group * PAIR, (group + 1) * PAIR)
            change = gathered[pl.ds(group, LANES, stride=groups), :].T[:PAIR]
            advected = spec_ref[rows, columns] + per_bin(speed_ref, group) * change
            growth = per_bin(coef_ref, group) * pushed - per_bin(loss_ref, group)
            result[block, rows, :] = advected * jnp.exp(growth)
        copy_out(block).start()
        high, low = split2(result[block])
        both = dot(kernel_both, high)
        stokes_ref[:, columns] = both[:depth] + both[depth:] + dot(kernel_high, low)

    @pl.loop(0, blocks)
    def _(block):
        copy_out(block).wait()


def advance(index, speed, coef, loss, spectrum, prev, nxt, edges, air, kernel):
    bins, points = spectrum.shape
    slots = edges.shape[0] // 2
    groups = bins // PAIR
    weight, facing = direction_constants(slots)
    rows = (points + prev.shape[1] + nxt.shape[1]) * groups
    return pl.pallas_call(
        functools.partial(advance_kernel, unroll=16),
        in_specs=[SMEM] * 4 + [VMEM] * 8,
        out_specs=[ANY, VMEM],
        out_shape=[
            jax.ShapeDtypeStruct((bins, points), F32),
            jax.ShapeDtypeStruct((kernel.shape[0], points), F32),
        ],
        scratch_shapes=[
            pltpu.VMEM((rows + 8, LANES), F32),
            pltpu.VMEM((slots, LANES + 8, LANES), F32),
            pltpu.VMEM((LANES * groups, LANES), F32),
            pltpu.VMEM((points // LANES, bins, LANES), F32),
            pltpu.SemaphoreType.DMA((points // LANES,)),
        ],
        compiler_params=params(40),
    )(index, speed, coef, loss, spectrum, prev, nxt, edges, air, weight, facing, kernel)


def regrid_kernel(slot_ref, stokes_ref, high_ref, low_ref, out_ref, *, block_rows):
    depth = stokes_ref.shape[0]
    out_ref[...] = jnp.zeros(out_ref.shape, F32)
    lower = lax.broadcasted_iota(jnp.int32, (depth, LANES), 1) < block_rows
    for pair in range(stokes_ref.shape[1] // LANES):
        columns = slice(pair * LANES, (pair + 1) * LANES)
        part = stokes_ref[:, columns]
        both = jnp.concatenate([jnp.where(lower, part, 0.0), jnp.where(lower, 0.0, part)], 0)
        high, low = split2(both)
        terms = (
            dot(high, high_ref[columns, :])
            + dot(low, high_ref[columns, :])
            + dot(high, low_ref[columns, :])
        )
        for half in range(2):
            slot = slot_ref[2 * pair + half]
            out_ref[slot] = out_ref[slot] + terms[half * depth : (half + 1) * depth]


def regrid(slots, stokes, high, low, count, block_rows):
    depth = stokes.shape[0]
    return pl.pallas_call(
        functools.partial(regrid_kernel, block_rows=block_rows),
        in_specs=[SMEM, VMEM, VMEM, VMEM],
        out_specs=VMEM,
        out_shape=jax.ShapeDtypeStruct((count, depth, LANES), F32),
        compiler_params=params(30),
    )(slots, stokes, high, low)


def swap(value, axis, bit):
    count = lax.axis_size(axis)
    return lax.ppermute(value, axis, [(i, i ^ bit) for i in range(count)])


def sum_over(value, axis):
    count = lax.axis_size(axis)
    me = lax.axis_index(axis)
    half = value.shape[1] // 2
    odd = (me & 1) == 1
    left, right = value[:, :half], value[:, half:]
    mine = jnp.where(odd, right, left) + swap(jnp.where(odd, left, right), axis, 1)
    bit = 2
    while bit < count:
        mine = mine + swap(mine, axis, bit)
        bit *= 2
    other = swap(mine, axis, 1)
    return jnp.concatenate([jnp.where(odd, other, mine), jnp.where(odd, mine, other)], 1)


def scatter_sum(parts, axis, bits):
    count = parts.shape[0]
    rest = parts.reshape((2,) * len(bits) + parts.shape[1:])
    for position, bit in enumerate(bits):
        live = sorted(bits[position:], reverse=True)
        dimension = live.index(bit)
        keep = lax.index_in_dim(rest, 0, dimension, keepdims=False)
        send = lax.index_in_dim(rest, 1, dimension, keepdims=False)
        rest = keep + swap(send, axis, bit)
    return rest


def shift(value, axis, steps):
    count = lax.axis_size(axis)
    leading, last = (max(0, -steps), min(count, count - steps))
    return lax.ppermute(value, axis, [(source, source + steps) for source in range(leading, last)])


def body(
    spectrum,
    edge_vectors,
    neighbours,
    halo_lists,
    group_speed,
    input_coef,
    dissipation,
    friction,
    wind_dir,
    drift_kernel,
    block_tile,
    block_weights,
):
    n_wave = lax.axis_size("wave")
    n_group = lax.axis_size("grp")
    to_next, to_prev = pick_halo(spectrum, halo_lists)
    from_prev = shift(to_next, "wave", 1)
    from_next = shift(to_prev, "wave", -1)
    slots = neighbours.shape[0]
    groups = spectrum.shape[0] // PAIR
    index = (neighbours * groups).T.reshape(-1)
    air = jnp.stack([jnp.cos(wind_dir), jnp.sin(wind_dir), friction])
    edges = edge_vectors.reshape(2 * slots, -1)
    updated, stokes = advance(
        index, group_speed, input_coef, dissipation, spectrum, from_prev, from_next, edges, air, drift_kernel
    )
    stokes = sum_over(stokes, "grp")
    blocks, block_rows, tile_cells = block_weights.shape
    cells = tile_cells // n_group
    mine = lax.dynamic_slice_in_dim(block_weights, lax.axis_index("grp") * cells, cells, 2)
    mine = mine.reshape(blocks * block_rows, cells)
    rounded = lax.reduce_precision(mine, 8, 7)
    high, low = rounded.astype(BF), (mine - rounded).astype(BF)
    relative = (block_tile // TPW) ^ lax.axis_index("wave")
    depth = drift_kernel.shape[0]
    parts = regrid(relative * TPW + block_tile % TPW, stokes, high, low, n_wave * TPW, block_rows)
    bits = [1 << b for b in range(n_wave.bit_length() - 1)]
    drift = scatter_sum(parts.reshape(n_wave, TPW, depth, cells), "wave", bits)
    return updated, drift


def solution(mesh):
    in_specs = (
        P("grp", "wave"),
        P(None, None, "wave"),
        P(None, "wave"),
        P(None, "wave", None),
        P("grp"),
        P("grp"),
        P("grp"),
        P("wave"),
        P("wave"),
        P(None, "grp"),
        P("wave"),
        P("wave", None, None),
    )
    out_specs = (P("grp", "wave"), P("wave", None, "grp"))
    return jax.shard_map(body, mesh=mesh, in_specs=in_specs, out_specs=out_specs, check_vma=False)
```

```python
import functools
import math

import jax
import jax.numpy as jnp
import ml_dtypes
import numpy as np
from jax import lax
from jax.experimental import pallas as pl
from jax.experimental.pallas import tpu as pltpu
from jax.sharding import PartitionSpec as P

ND = 36
TPW = 4
LANES = 128
UNROLL = 16
PAIR = 2 * ND
BF = jnp.bfloat16
F32 = jnp.float32
VMEM = pl.BlockSpec(memory_space=pltpu.VMEM)
SMEM = pl.BlockSpec(memory_space=pltpu.SMEM)
ANY = pl.BlockSpec(memory_space=pl.ANY)


def params(mib):
    return pltpu.CompilerParams(vmem_limit_bytes=mib << 20)


def split2(x):
    high = x.astype(BF)
    return high, (x - high.astype(F32)).astype(BF)


def dot(a, b):
    return jnp.dot(a, b, preferred_element_type=F32)


def direction_constants(slots):
    theta = np.arange(ND) * (2.0 * math.pi / ND)
    cosine, sine = np.cos(theta), np.sin(theta)
    table = np.zeros((2, slots, slots, LANES), np.float32)
    for slot in range(slots):
        for half in range(2):
            table[0, slot, slot, half * ND : (half + 1) * ND] = -cosine
            table[1, slot, slot, half * ND : (half + 1) * ND] = -sine
    table = table.reshape(2 * slots, slots * LANES)
    high = table.astype(ml_dtypes.bfloat16)
    low = (table - high.astype(np.float32)).astype(ml_dtypes.bfloat16)
    rows = np.stack([np.tile(cosine, 2), np.tile(sine, 2)]).astype(np.float32)
    facing = np.broadcast_to(rows[:, :, None], (2, PAIR, LANES))
    return np.concatenate([high, low, high], 0), np.ascontiguousarray(facing)


def vmem(shape, dtype=F32):
    return pltpu.VMEM(shape, dtype)


def in_hbm(*arrays):
    return [pltpu.with_memory_space_constraint(array, pltpu.HBM) for array in arrays]


def start_all(sources, targets, sems):
    copies = [
        pltpu.make_async_copy(source, target, sems.at[number])
        for number, (source, target) in enumerate(zip(sources, targets))
    ]
    for copy in copies:
        copy.start()
    return copies


def pick_kernel(lists_hbm, spec_hbm, spec_ref, next_ref, prev_ref, lists_ref, sems, small_sems):
    points = spec_ref.shape[1]
    chunks = sems.shape[0]
    width = points // chunks
    copies = []
    for chunk in range(chunks):
        columns = pl.ds(chunk * width, width)
        copies.append(
            pltpu.make_async_copy(
                spec_hbm.at[:, columns], spec_ref.at[:, columns], sems.at[chunk]
            )
        )
    (lists_copy,) = start_all([lists_hbm], [lists_ref], small_sems)
    for copy in copies:
        copy.start()
    lists_copy.wait()
    count = next_ref.shape[1]
    lists = jnp.concatenate([lists_ref[0], lists_ref[1]], 1)
    total = None
    for chunk in range(chunks):
        copies[chunk].wait()
        part = spec_ref[:, chunk * width : (chunk + 1) * width]
        first = part.astype(BF)
        rest = part - first.astype(F32)
        second = rest.astype(BF)
        third = (rest - second.astype(F32)).astype(BF)
        ids = lax.broadcasted_iota(jnp.int32, (width, 2 * count), 0) + chunk * width
        chosen = jnp.where(ids == lists, 1.0, 0.0).astype(BF)
        found = dot(first, chosen) + (dot(second, chosen) + dot(third, chosen))
        total = found if total is None else total + found
    next_ref[...] = total[:, :count]
    prev_ref[...] = total[:, count:]


def pick_halo(spectrum, lists):
    bins, points = spectrum.shape
    halo = jax.ShapeDtypeStruct((bins, lists.shape[-1]), F32)
    return pl.pallas_call(
        pick_kernel,
        in_specs=[ANY, ANY],
        out_specs=[VMEM] * 3,
        out_shape=[vmem((bins, points)), halo, halo],
        scratch_shapes=[
            pltpu.VMEM(lists.shape, jnp.int32),
            pltpu.SemaphoreType.DMA((8,)),
            pltpu.SemaphoreType.DMA((1,)),
        ],
        compiler_params=params(8),
    )(*in_hbm(lists, spectrum))


def prepare_kernel(*refs):
    spec_ref, operands = refs[0], refs[1:9]
    table, inflow, gain, index_out = refs[9:13]
    scratch, (turn, sems, index_sem) = refs[13:21], refs[21:]
    copies = start_all(operands, scratch, sems)
    coef_ref, loss_ref, edge_ref, wind_ref, friction_ref, weight_ref, facing_ref, index_ref = scratch
    bins, points = gain.shape
    groups = bins // PAIR
    slots = inflow.shape[0]
    filler = jnp.zeros((LANES - PAIR, LANES), F32)

    @pl.loop(0, points // LANES)
    def _(block):
        columns = pl.ds(pl.multiple_of(block * LANES, LANES), LANES)
        for group in range(groups):
            part = spec_ref[group * PAIR : (group + 1) * PAIR, columns]
            rows = pl.ds(block * (LANES * groups) + group, LANES, stride=groups)
            table[rows, :] = jnp.concatenate([part, filler], 0).T

    for copy in copies:
        copy.wait()
    index_ref[...] = index_ref[...] * groups
    index_copy = pltpu.make_async_copy(index_ref, index_out, index_sem)
    index_copy.start()
    lower = lax.broadcasted_iota(jnp.int32, (PAIR, LANES), 0) < ND

    def per_bin(ref, group):
        return jnp.where(lower, ref[2 * group], ref[2 * group + 1])

    coef = [per_bin(coef_ref, group) for group in range(groups)]
    loss = [per_bin(loss_ref, group) for group in range(groups)]
    turn[0] = jnp.cos(wind_ref[...])
    turn[1] = jnp.sin(wind_ref[...])

    @pl.loop(0, points // LANES)
    def _(block):
        base = pl.multiple_of(block * LANES, LANES)
        columns = pl.ds(base, LANES)
        edge_high, edge_low = split2(edge_ref[:, columns])
        left = jnp.concatenate([edge_high, edge_high, edge_low], 0)
        weights = lax.dot_general(
            left, weight_ref[...], (((0,), (0,)), ((), ())), preferred_element_type=F32
        )
        for slot in range(slots):
            factor = jnp.maximum(weights[:, slot * LANES : (slot + 1) * LANES], 0.0)
            inflow[slot, pl.ds(base, LANES), :] = factor
        row = pl.ds(block, 1)
        facing = facing_ref[0] * turn[0, row, :] + facing_ref[1] * turn[1, row, :]
        pushed = jnp.maximum(facing, 0.0) * friction_ref[row, :]
        for group in range(groups):
            gain[group * PAIR : (group + 1) * PAIR, columns] = jnp.exp(
                coef[group] * pushed - loss[group]
            )

    index_copy.wait()


def prepare(spectrum, coef, loss, edges, wind, friction, index, rows):
    bins, points = spectrum.shape
    slots = edges.shape[0] // 2
    weight, facing = direction_constants(slots)
    shape = (points // LANES, LANES)
    operands = [edges, wind.reshape(shape), friction.reshape(shape), weight, facing, index]
    operands = [jnp.asarray(operand) for operand in operands]
    return pl.pallas_call(
        prepare_kernel,
        in_specs=[VMEM] + [ANY] * 8,
        out_specs=[VMEM, VMEM, VMEM, ANY],
        out_shape=[
            vmem((rows, LANES)),
            vmem((slots, points + 8, LANES)),
            vmem((bins, points)),
            pltpu.HBM(index.shape, index.dtype),
        ],
        scratch_shapes=[
            pltpu.SMEM(coef.shape, F32),
            pltpu.SMEM(loss.shape, F32),
            *[pltpu.VMEM(operand.shape, operand.dtype) for operand in operands],
            pltpu.VMEM((2, *shape), F32),
            pltpu.SemaphoreType.DMA((8,)),
            pltpu.SemaphoreType.DMA(()),
        ],
        compiler_params=params(6),
    )(spectrum, *in_hbm(coef, loss, *operands))


def advance_kernel(
    speed_hbm,
    index_hbm,
    kernel_hbm,
    table_in,
    inflow,
    spec_ref,
    gain_ref,
    prev_ref,
    next_ref,
    updated_ref,
    stokes_ref,
    table,
    speed_ref,
    kernel_ref,
    index_ref,
    gathered,
    result,
    sems,
    index_sems,
    small_sems,
    *,
    unroll,
):
    bins, points = spec_ref.shape
    groups = bins // PAIR
    slots = inflow.shape[0]
    halo = prev_ref.shape[1]
    blocks = points // LANES
    filler = jnp.zeros((LANES - PAIR, LANES), F32)

    def fetch(block):
        return pltpu.make_async_copy(index_hbm.at[block], index_ref.at[block], index_sems.at[block])

    @pl.loop(0, blocks)
    def _(block):
        fetch(block).start()

    small = start_all([speed_hbm, kernel_hbm], [speed_ref, kernel_ref], small_sems)

    for number, ref in enumerate((prev_ref, next_ref)):
        for group in range(groups):
            part = jnp.concatenate([ref[group * PAIR : (group + 1) * PAIR, :], filler], 0).T
            start = (points + number * halo) * groups + group
            table[pl.ds(start, halo, stride=groups), :] = part

    for copy in small:
        copy.wait()
    kernel_high, kernel_low = split2(kernel_ref[...])
    kernel_both = jnp.concatenate([kernel_high, kernel_low], 0)
    depth = kernel_ref.shape[0]
    lower = lax.broadcasted_iota(jnp.int32, (PAIR, LANES), 0) < ND

    def copy_out(block):
        columns = pl.ds(pl.multiple_of(block * LANES, LANES), LANES)
        return pltpu.make_async_copy(
            result.at[block], updated_ref.at[:, columns], sems.at[block]
        )

    @pl.loop(0, blocks)
    def _(block):
        base = pl.multiple_of(block * LANES, LANES)
        columns = pl.ds(base, LANES)
        fetch(block).wait()

        @pl.loop(0, LANES // unroll)
        def _(chunk):
            first = pl.multiple_of(chunk * unroll, unroll)
            picks = [
                index_ref.at[block, slot, pl.ds(first, unroll)]
                for slot in range(slots)
            ]
            for u in range(unroll):
                point = base + first + u
                own = table[pl.ds(point * groups, groups), :]
                terms = []
                for slot in range(slots):
                    upwind = table[pl.ds(picks[slot][u], groups), :]
                    factor = inflow[slot, pl.ds(point, groups, stride=0), :]
                    terms.append(factor * (upwind - own))
                while len(terms) > 1:
                    terms = [a + b for a, b in zip(terms[::2], terms[1::2])]
                gathered[pl.ds((first + u) * groups, groups), :] = terms[0]

        for group in range(groups):
            rows = slice(group * PAIR, (group + 1) * PAIR)
            change = gathered[pl.ds(group, LANES, stride=groups), :].T[:PAIR]
            speed = jnp.where(lower, speed_ref[2 * group], speed_ref[2 * group + 1])
            advected = spec_ref[rows, columns] + speed * change
            result[block, rows, :] = advected * gain_ref[rows, columns]
        copy_out(block).start()
        high, low = split2(result[block])
        both = dot(kernel_both, high)
        stokes_ref[:, columns] = both[:depth] + both[depth:] + dot(kernel_high, low)

    @pl.loop(0, blocks)
    def _(block):
        copy_out(block).wait()


def advance(speed, index, table, inflow, spectrum, gain, prev, nxt, kernel):
    bins, points = spectrum.shape
    groups = bins // PAIR
    blocks = points // LANES
    return pl.pallas_call(
        functools.partial(advance_kernel, unroll=UNROLL),
        in_specs=[ANY] * 3 + [VMEM] * 6,
        out_specs=[ANY, VMEM, VMEM],
        out_shape=[
            jax.ShapeDtypeStruct((bins, points), F32),
            jax.ShapeDtypeStruct((kernel.shape[0], points), F32),
            vmem(table.shape),
        ],
        input_output_aliases={3: 2},
        scratch_shapes=[
            pltpu.SMEM(speed.shape, F32),
            pltpu.VMEM(kernel.shape, F32),
            pltpu.SMEM(index.shape, jnp.int32),
            pltpu.VMEM((LANES * groups, LANES), F32),
            pltpu.VMEM((blocks, bins, LANES), F32),
            pltpu.SemaphoreType.DMA((blocks,)),
            pltpu.SemaphoreType.DMA((blocks,)),
            pltpu.SemaphoreType.DMA((2,)),
        ],
        compiler_params=params(10),
    )(*in_hbm(speed, index, kernel), table, inflow, spectrum, gain, prev, nxt)


def regrid_kernel(slot_ref, stokes_ref, high_ref, low_ref, out_ref, *, block_rows):
    depth = stokes_ref.shape[0]
    out_ref[...] = jnp.zeros(out_ref.shape, F32)
    lower = lax.broadcasted_iota(jnp.int32, (depth, LANES), 1) < block_rows
    for pair in range(stokes_ref.shape[1] // LANES):
        columns = slice(pair * LANES, (pair + 1) * LANES)
        part = stokes_ref[:, columns]
        both = jnp.concatenate([jnp.where(lower, part, 0.0), jnp.where(lower, 0.0, part)], 0)
        high, low = split2(both)
        terms = (
            dot(high, high_ref[columns, :])
            + dot(low, high_ref[columns, :])
            + dot(high, low_ref[columns, :])
        )
        for half in range(2):
            slot = slot_ref[2 * pair + half]
            out_ref[slot] = out_ref[slot] + terms[half * depth : (half + 1) * depth]


def regrid(slots, stokes, high, low, count, block_rows):
    depth = stokes.shape[0]
    return pl.pallas_call(
        functools.partial(regrid_kernel, block_rows=block_rows),
        in_specs=[SMEM, VMEM, VMEM, VMEM],
        out_specs=VMEM,
        out_shape=jax.ShapeDtypeStruct((count, depth, LANES), F32),
        compiler_params=params(4),
    )(slots, stokes, high, low)


def swap(value, axis, bit):
    count = lax.axis_size(axis)
    return lax.ppermute(value, axis, [(i, i ^ bit) for i in range(count)])


def sum_over(value, axis):
    count = lax.axis_size(axis)
    me = lax.axis_index(axis)
    half = value.shape[1] // 2
    odd = (me & 1) == 1
    left, right = value[:, :half], value[:, half:]
    mine = jnp.where(odd, right, left) + swap(jnp.where(odd, left, right), axis, 1)
    bit = 2
    while bit < count:
        mine = mine + swap(mine, axis, bit)
        bit *= 2
    other = swap(mine, axis, 1)
    return jnp.concatenate([jnp.where(odd, other, mine), jnp.where(odd, mine, other)], 1)


def places(relative, bits):
    total = jnp.zeros_like(relative)
    for bit in bits:
        total = 2 * total + jnp.where((relative & bit) != 0, 1, 0)
    return total


def exchange(value, even_bit, odd_bit):
    waves, groups = lax.axis_size("wave"), lax.axis_size("grp")
    pairs = [
        (w * groups + g, (w ^ (odd_bit if g % 2 else even_bit)) * groups + g)
        for w in range(waves)
        for g in range(groups)
    ]
    return lax.ppermute(value, ("wave", "grp"), pairs)


def scatter_sum(parts, bits, other_bits):
    for bit, other in zip(bits, other_bits):
        half = parts.shape[0] // 2
        parts = parts[:half] + exchange(parts[half:], bit, other)
    return parts[0]


def shift(value, axis, steps):
    count = lax.axis_size(axis)
    leading, last = (max(0, -steps), min(count, count - steps))
    return lax.ppermute(value, axis, [(source, source + steps) for source in range(leading, last)])


def body(
    spectrum,
    edge_vectors,
    neighbours,
    halo_lists,
    group_speed,
    input_coef,
    dissipation,
    friction,
    wind_dir,
    drift_kernel,
    block_tile,
    block_weights,
):
    n_wave = lax.axis_size("wave")
    n_group = lax.axis_size("grp")
    bins, points = spectrum.shape
    groups = bins // PAIR
    slots = neighbours.shape[0]
    rows = (points + 2 * halo_lists.shape[-1]) * groups
    spectrum, to_next, to_prev = pick_halo(spectrum, halo_lists)
    from_prev = shift(to_next, "wave", 1)
    from_next = shift(to_prev, "wave", -1)
    index = neighbours.reshape(slots, points // LANES, LANES).transpose(1, 0, 2)
    edges = edge_vectors.reshape(2 * slots, points)
    table, inflow, gain, index = prepare(
        spectrum, input_coef, dissipation, edges, wind_dir, friction, index, rows
    )
    updated, stokes, _ = advance(
        group_speed, index, table, inflow, spectrum, gain, from_prev, from_next, drift_kernel
    )
    stokes = sum_over(stokes, "grp")
    blocks, block_rows, tile_cells = block_weights.shape
    cells = tile_cells // n_group
    mine = lax.dynamic_slice_in_dim(block_weights, lax.axis_index("grp") * cells, cells, 2)
    mine = mine.reshape(blocks * block_rows, cells)
    rounded = lax.reduce_precision(mine, 8, 7)
    high, low = rounded.astype(BF), (mine - rounded).astype(BF)
    relative = (block_tile // TPW) ^ lax.axis_index("wave")
    tile = block_tile % TPW
    depth = drift_kernel.shape[0]
    bits = [1 << b for b in range(n_wave.bit_length() - 1)]
    other_bits = bits[1::-1] + bits[2:]
    odd = lax.axis_index("grp") % 2 == 1
    place = jnp.where(odd, places(relative, other_bits), places(relative, bits))
    parts = regrid(place * TPW + tile, stokes, high, low, n_wave * TPW, block_rows)
    drift = scatter_sum(parts.reshape(n_wave, TPW, depth, cells), bits, other_bits)
    return updated, drift


def solution(mesh):
    in_specs = (
        P("grp", "wave"),
        P(None, None, "wave"),
        P(None, "wave"),
        P(None, "wave", None),
        P("grp"),
        P("grp"),
        P("grp"),
        P("wave"),
        P("wave"),
        P(None, "grp"),
        P("wave"),
        P("wave", None, None),
    )
    out_specs = (P("grp", "wave"), P("wave", None, "grp"))
    return jax.shard_map(body, mesh=mesh, in_specs=in_specs, out_specs=out_specs, check_vma=False)
```

```python
import functools
import math

import jax
import jax.numpy as jnp
import ml_dtypes
import numpy as np
from jax import lax
from jax.experimental import pallas as pl
from jax.experimental.pallas import tpu as pltpu
from jax.sharding import PartitionSpec as P

ND = 36
TPW = 4
LANES = 128
UNROLL = 128
WIDTH = 512
PAIR = 2 * ND
BF = jnp.bfloat16
F32 = jnp.float32
VMEM = pl.BlockSpec(memory_space=pltpu.VMEM)
SMEM = pl.BlockSpec(memory_space=pltpu.SMEM)
ANY = pl.BlockSpec(memory_space=pl.ANY)


def params(mib):
    return pltpu.CompilerParams(vmem_limit_bytes=mib << 20)


def split2(x):
    high = x.astype(BF)
    return high, (x - high.astype(F32)).astype(BF)


def dot(a, b):
    return jnp.dot(a, b, preferred_element_type=F32)


def direction_constants(slots):
    theta = np.arange(ND) * (2.0 * math.pi / ND)
    cosine, sine = np.cos(theta), np.sin(theta)
    table = np.zeros((2, slots, slots, LANES), np.float32)
    for slot in range(slots):
        for half in range(2):
            table[0, slot, slot, half * ND : (half + 1) * ND] = -cosine
            table[1, slot, slot, half * ND : (half + 1) * ND] = -sine
    table = table.reshape(2 * slots, slots * LANES)
    high = table.astype(ml_dtypes.bfloat16)
    low = (table - high.astype(np.float32)).astype(ml_dtypes.bfloat16)
    rows = np.stack([np.tile(cosine, 2), np.tile(sine, 2)]).astype(np.float32)
    facing = np.broadcast_to(rows[:, :, None], (2, PAIR, LANES))
    return np.concatenate([high, low, high], 0), np.ascontiguousarray(facing)


def vmem(shape, dtype=F32):
    return pltpu.VMEM(shape, dtype)


def in_hbm(*arrays):
    return [pltpu.with_memory_space_constraint(array, pltpu.HBM) for array in arrays]


def start_all(sources, targets, sems):
    copies = [
        pltpu.make_async_copy(source, target, sems.at[number])
        for number, (source, target) in enumerate(zip(sources, targets))
    ]
    for copy in copies:
        copy.start()
    return copies


def pick_kernel(lists_hbm, spec_hbm, spec_ref, next_ref, prev_ref, lists_ref, sems, small_sems):
    points = spec_ref.shape[1]
    chunks = sems.shape[0]
    width = points // chunks
    copies = []
    for chunk in range(chunks):
        columns = pl.ds(chunk * width, width)
        copies.append(
            pltpu.make_async_copy(
                spec_hbm.at[:, columns], spec_ref.at[:, columns], sems.at[chunk]
            )
        )
    (lists_copy,) = start_all([lists_hbm], [lists_ref], small_sems)
    for copy in copies:
        copy.start()
    lists_copy.wait()
    count = next_ref.shape[1]
    lists = jnp.concatenate([lists_ref[0], lists_ref[1]], 1)
    total = None
    for chunk in range(chunks):
        copies[chunk].wait()
        part = spec_ref[:, chunk * width : (chunk + 1) * width]
        first, second = split2(part)
        ids = lax.broadcasted_iota(jnp.int32, (width, 2 * count), 0) + chunk * width
        chosen = jnp.where(ids == lists, 1.0, 0.0).astype(BF)
        found = dot(first, chosen) + dot(second, chosen)
        total = found if total is None else total + found
    next_ref[...] = total[:, :count]
    prev_ref[...] = total[:, count:]


def pick_halo(spectrum, lists):
    bins, points = spectrum.shape
    halo = jax.ShapeDtypeStruct((bins, lists.shape[-1]), F32)
    return pl.pallas_call(
        pick_kernel,
        in_specs=[ANY, ANY],
        out_specs=[VMEM] * 3,
        out_shape=[vmem((bins, points)), halo, halo],
        scratch_shapes=[
            pltpu.VMEM(lists.shape, jnp.int32),
            pltpu.SemaphoreType.DMA((4,)),
            pltpu.SemaphoreType.DMA((1,)),
        ],
        compiler_params=params(8),
    )(*in_hbm(lists, spectrum))


def prepare_kernel(*refs):
    spec_ref, operands = refs[0], refs[1:9]
    table, inflow, gain, index_out = refs[9:13]
    scratch, (turn, sems, index_sem) = refs[13:21], refs[21:]
    copies = start_all(operands, scratch, sems)
    coef_ref, loss_ref, edge_ref, wind_ref, friction_ref, weight_ref, facing_ref, index_ref = scratch
    bins, points = gain.shape
    groups = bins // PAIR
    slots = inflow.shape[0]
    filler = jnp.zeros((LANES - PAIR, LANES), F32)

    @pl.loop(0, points // LANES, unroll=8)
    def _(block):
        columns = pl.ds(pl.multiple_of(block * LANES, LANES), LANES)
        for group in range(groups):
            part = spec_ref[group * PAIR : (group + 1) * PAIR, columns]
            rows = pl.ds(block * (LANES * groups) + group, LANES, stride=groups)
            table[rows, :] = jnp.concatenate([part, filler], 0).T

    for copy in copies:
        copy.wait()
    index_ref[...] = index_ref[...] * groups
    index_copy = pltpu.make_async_copy(index_ref, index_out, index_sem)
    index_copy.start()
    lower = lax.broadcasted_iota(jnp.int32, (PAIR, LANES), 0) < ND

    def per_bin(ref, group):
        return jnp.where(lower, ref[2 * group], ref[2 * group + 1])

    coef = [per_bin(coef_ref, group) for group in range(groups)]
    loss = [per_bin(loss_ref, group) for group in range(groups)]
    turn[0] = jnp.cos(wind_ref[...])
    turn[1] = jnp.sin(wind_ref[...])

    @pl.loop(0, points // LANES, unroll=8)
    def _(block):
        base = pl.multiple_of(block * LANES, LANES)
        columns = pl.ds(base, LANES)
        edge_high, edge_low = split2(edge_ref[:, columns])
        left = jnp.concatenate([edge_high, edge_high, edge_low], 0)
        weights = lax.dot_general(
            left, weight_ref[...], (((0,), (0,)), ((), ())), preferred_element_type=F32
        )
        for slot in range(slots):
            factor = jnp.maximum(weights[:, slot * LANES : (slot + 1) * LANES], 0.0)
            inflow[slot, pl.ds(base, LANES), :] = factor
        row = pl.ds(block, 1)
        facing = facing_ref[0] * turn[0, row, :] + facing_ref[1] * turn[1, row, :]
        pushed = jnp.maximum(facing, 0.0) * friction_ref[row, :]
        for group in range(groups):
            gain[group * PAIR : (group + 1) * PAIR, columns] = jnp.exp(
                coef[group] * pushed - loss[group]
            )

    index_copy.wait()


def prepare(spectrum, coef, loss, edges, wind, friction, index, rows):
    bins, points = spectrum.shape
    slots = edges.shape[0] // 2
    weight, facing = direction_constants(slots)
    shape = (points // LANES, LANES)
    operands = [edges, wind.reshape(shape), friction.reshape(shape), weight, facing, index]
    operands = [jnp.asarray(operand) for operand in operands]
    return pl.pallas_call(
        prepare_kernel,
        in_specs=[VMEM] + [ANY] * 8,
        out_specs=[VMEM, VMEM, VMEM, ANY],
        out_shape=[
            vmem((rows, LANES)),
            vmem((slots, points + 8, LANES)),
            vmem((bins, points)),
            pltpu.HBM(index.shape, index.dtype),
        ],
        scratch_shapes=[
            pltpu.SMEM(coef.shape, F32),
            pltpu.SMEM(loss.shape, F32),
            *[pltpu.VMEM(operand.shape, operand.dtype) for operand in operands],
            pltpu.VMEM((2, *shape), F32),
            pltpu.SemaphoreType.DMA((8,)),
            pltpu.SemaphoreType.DMA(()),
        ],
        compiler_params=params(6),
    )(spectrum, *in_hbm(coef, loss, *operands))


def advance_kernel(
    speed_hbm,
    index_hbm,
    kernel_hbm,
    table_in,
    inflow,
    spec_ref,
    gain_ref,
    prev_ref,
    next_ref,
    updated_ref,
    stokes_ref,
    table,
    speed_ref,
    kernel_ref,
    index_ref,
    gathered,
    result,
    sems,
    index_sems,
    small_sems,
    *,
    unroll,
):
    bins, points = spec_ref.shape
    groups = bins // PAIR
    slots = inflow.shape[0]
    halo = prev_ref.shape[1]
    blocks = points // LANES
    filler = jnp.zeros((LANES - PAIR, LANES), F32)

    def fetch(block):
        return pltpu.make_async_copy(index_hbm.at[block], index_ref.at[block], index_sems.at[block])

    @pl.loop(0, blocks)
    def _(block):
        fetch(block).start()

    small = start_all([speed_hbm, kernel_hbm], [speed_ref, kernel_ref], small_sems)

    for number, ref in enumerate((prev_ref, next_ref)):
        for group in range(groups):
            part = jnp.concatenate([ref[group * PAIR : (group + 1) * PAIR, :], filler], 0).T
            start = (points + number * halo) * groups + group
            table[pl.ds(start, halo, stride=groups), :] = part

    for copy in small:
        copy.wait()
    kernel_high, kernel_low = split2(kernel_ref[...])
    kernel_both = jnp.concatenate([kernel_high, kernel_low], 0)
    depth = kernel_ref.shape[0]
    lower = lax.broadcasted_iota(jnp.int32, (PAIR, LANES), 0) < ND

    width = result.shape[2]

    def copy_out(part, group):
        columns = pl.ds(pl.multiple_of(part * width, width), width)
        rows = pl.ds(group * PAIR, PAIR)
        return pltpu.make_async_copy(
            result.at[part, rows], updated_ref.at[rows, columns], sems.at[part, group]
        )

    def gather(block, start):
        fetch(block).wait()
        base = pl.multiple_of(block * LANES, LANES)

        @pl.loop(0, LANES // unroll)
        def _(chunk):
            first = pl.multiple_of(chunk * unroll, unroll)
            picks = [index_ref.at[block, slot, pl.ds(first, unroll)] for slot in range(slots)]
            for u in range(unroll):
                point = base + first + u
                own = table[pl.ds(point * groups, groups), :]
                terms = []
                for slot in range(slots):
                    upwind = table[pl.ds(picks[slot][u], groups), :]
                    factor = inflow[slot, pl.ds(point, groups, stride=0), :]
                    terms.append(factor * (upwind - own))
                while len(terms) > 1:
                    terms = [a + b for a, b in zip(terms[::2], terms[1::2])]
                gathered[pl.ds((start + first + u) * groups, groups), :] = terms[0]

    @pl.loop(0, points // width)
    def _(part):
        columns = pl.ds(pl.multiple_of(part * width, width), width)
        several = width // LANES

        @pl.loop(0, several)
        def _(step):
            gather(part * several + step, pl.multiple_of(step * LANES, LANES))

        for group in range(groups):
            rows = slice(group * PAIR, (group + 1) * PAIR)
            speed = jnp.where(lower, speed_ref[2 * group], speed_ref[2 * group + 1])
            for step in range(several):
                inner = slice(step * LANES, (step + 1) * LANES)
                outer = pl.ds(pl.multiple_of(part * width + step * LANES, LANES), LANES)
                picked = gathered[pl.ds(step * LANES * groups + group, LANES, stride=groups), :]
                advected = spec_ref[rows, outer] + speed * picked.T[:PAIR]
                result[part, rows, inner] = advected * gain_ref[rows, outer]
            copy_out(part, group).start()
        high, low = split2(result[part])
        both = dot(kernel_both, high)
        stokes_ref[:, columns] = both[:depth] + both[depth:] + dot(kernel_high, low)

    @pl.loop(0, points // width)
    def _(part):
        for group in range(groups):
            copy_out(part, group).wait()


def advance(speed, index, table, inflow, spectrum, gain, prev, nxt, kernel):
    bins, points = spectrum.shape
    groups = bins // PAIR
    blocks = points // LANES
    return pl.pallas_call(
        functools.partial(advance_kernel, unroll=UNROLL),
        in_specs=[ANY] * 3 + [VMEM] * 6,
        out_specs=[ANY, VMEM, VMEM],
        out_shape=[
            jax.ShapeDtypeStruct((bins, points), F32),
            jax.ShapeDtypeStruct((kernel.shape[0], points), F32),
            vmem(table.shape),
        ],
        input_output_aliases={3: 2},
        scratch_shapes=[
            pltpu.SMEM(speed.shape, F32),
            pltpu.VMEM(kernel.shape, F32),
            pltpu.SMEM(index.shape, jnp.int32),
            pltpu.VMEM((WIDTH * groups, LANES), F32),
            pltpu.VMEM((points // WIDTH, bins, WIDTH), F32),
            pltpu.SemaphoreType.DMA((points // WIDTH, groups)),
            pltpu.SemaphoreType.DMA((blocks,)),
            pltpu.SemaphoreType.DMA((2,)),
        ],
        compiler_params=params(10),
    )(*in_hbm(speed, index, kernel), table, inflow, spectrum, gain, prev, nxt)


def regrid_kernel(slot_ref, stokes_ref, high_ref, low_ref, out_ref, *, block_rows):
    depth = stokes_ref.shape[0]
    out_ref[...] = jnp.zeros(out_ref.shape, F32)
    lower = lax.broadcasted_iota(jnp.int32, (depth, LANES), 1) < block_rows
    for pair in range(stokes_ref.shape[1] // LANES):
        columns = slice(pair * LANES, (pair + 1) * LANES)
        part = stokes_ref[:, columns]
        both = jnp.concatenate([jnp.where(lower, part, 0.0), jnp.where(lower, 0.0, part)], 0)
        high, low = split2(both)
        terms = (
            dot(high, high_ref[columns, :])
            + dot(low, high_ref[columns, :])
            + dot(high, low_ref[columns, :])
        )
        for half in range(2):
            slot = slot_ref[2 * pair + half]
            out_ref[slot] = out_ref[slot] + terms[half * depth : (half + 1) * depth]


def regrid(slots, stokes, high, low, count, block_rows):
    depth = stokes.shape[0]
    return pl.pallas_call(
        functools.partial(regrid_kernel, block_rows=block_rows),
        in_specs=[SMEM, VMEM, VMEM, VMEM],
        out_specs=VMEM,
        out_shape=jax.ShapeDtypeStruct((count, depth, LANES), F32),
        compiler_params=params(4),
    )(slots, stokes, high, low)


def swap(value, axis, bit):
    count = lax.axis_size(axis)
    return lax.ppermute(value, axis, [(i, i ^ bit) for i in range(count)])


def sum_over(value, axis):
    count = lax.axis_size(axis)
    me = lax.axis_index(axis)
    half = value.shape[1] // 2
    odd = (me & 1) == 1
    left, right = value[:, :half], value[:, half:]
    mine = jnp.where(odd, right, left) + swap(jnp.where(odd, left, right), axis, 1)
    bit = 2
    while bit < count:
        mine = mine + swap(mine, axis, bit)
        bit *= 2
    other = swap(mine, axis, 1)
    return jnp.concatenate([jnp.where(odd, other, mine), jnp.where(odd, mine, other)], 1)


def places(relative, bits):
    total = jnp.zeros_like(relative)
    for bit in bits:
        total = 2 * total + jnp.where((relative & bit) != 0, 1, 0)
    return total


def exchange(value, even_bit, odd_bit):
    waves, groups = lax.axis_size("wave"), lax.axis_size("grp")
    pairs = [
        (w * groups + g, (w ^ (odd_bit if g % 2 else even_bit)) * groups + g)
        for w in range(waves)
        for g in range(groups)
    ]
    return lax.ppermute(value, ("wave", "grp"), pairs)


def scatter_sum(parts, bits, other_bits):
    for bit, other in zip(bits, other_bits):
        half = parts.shape[0] // 2
        parts = parts[:half] + exchange(parts[half:], bit, other)
    return parts[0]


def shift(value, axis, steps):
    count = lax.axis_size(axis)
    leading, last = (max(0, -steps), min(count, count - steps))
    return lax.ppermute(value, axis, [(source, source + steps) for source in range(leading, last)])


def body(
    spectrum,
    edge_vectors,
    neighbours,
    halo_lists,
    group_speed,
    input_coef,
    dissipation,
    friction,
    wind_dir,
    drift_kernel,
    block_tile,
    block_weights,
):
    n_wave = lax.axis_size("wave")
    n_group = lax.axis_size("grp")
    bins, points = spectrum.shape
    groups = bins // PAIR
    slots = neighbours.shape[0]
    rows = (points + 2 * halo_lists.shape[-1]) * groups
    spectrum, to_next, to_prev = pick_halo(spectrum, halo_lists)
    from_prev = shift(to_next, "wave", 1)
    from_next = shift(to_prev, "wave", -1)
    index = neighbours.reshape(slots, points // LANES, LANES).transpose(1, 0, 2)
    edges = edge_vectors.reshape(2 * slots, points)
    table, inflow, gain, index = prepare(
        spectrum, input_coef, dissipation, edges, wind_dir, friction, index, rows
    )
    updated, stokes, _ = advance(
        group_speed, index, table, inflow, spectrum, gain, from_prev, from_next, drift_kernel
    )
    stokes = sum_over(stokes, "grp")
    blocks, block_rows, tile_cells = block_weights.shape
    cells = tile_cells // n_group
    mine = lax.dynamic_slice_in_dim(block_weights, lax.axis_index("grp") * cells, cells, 2)
    mine = mine.reshape(blocks * block_rows, cells)
    rounded = lax.reduce_precision(mine, 8, 7)
    high, low = rounded.astype(BF), (mine - rounded).astype(BF)
    relative = (block_tile // TPW) ^ lax.axis_index("wave")
    tile = block_tile % TPW
    depth = drift_kernel.shape[0]
    bits = [1 << b for b in range(n_wave.bit_length() - 1)]
    other_bits = bits[1::-1] + bits[2:]
    odd = lax.axis_index("grp") % 2 == 1
    place = jnp.where(odd, places(relative, other_bits), places(relative, bits))
    parts = regrid(place * TPW + tile, stokes, high, low, n_wave * TPW, block_rows)
    drift = scatter_sum(parts.reshape(n_wave, TPW, depth, cells), bits, other_bits)
    return updated, drift


def solution(mesh):
    in_specs = (
        P("grp", "wave"),
        P(None, None, "wave"),
        P(None, "wave"),
        P(None, "wave", None),
        P("grp"),
        P("grp"),
        P("grp"),
        P("wave"),
        P("wave"),
        P(None, "grp"),
        P("wave"),
        P("wave", None, None),
    )
    out_specs = (P("grp", "wave"), P("wave", None, "grp"))
    return jax.shard_map(body, mesh=mesh, in_specs=in_specs, out_specs=out_specs, check_vma=False)
```

```python
import functools
import math

import jax
import jax.numpy as jnp
import ml_dtypes
import numpy as np
from jax import lax
from jax.experimental import pallas as pl
from jax.experimental.pallas import tpu as pltpu
from jax.sharding import PartitionSpec as P

ND = 36
TPW = 4
LANES = 128
UNROLL = 128
WIDTH = 1024
PAIR = 2 * ND
BF = jnp.bfloat16
F32 = jnp.float32
VMEM = pl.BlockSpec(memory_space=pltpu.VMEM)
SMEM = pl.BlockSpec(memory_space=pltpu.SMEM)
ANY = pl.BlockSpec(memory_space=pl.ANY)


def params(mib):
    return pltpu.CompilerParams(vmem_limit_bytes=mib << 20)


def split2(x):
    high = x.astype(BF)
    return high, (x - high.astype(F32)).astype(BF)


def dot(a, b):
    return jnp.dot(a, b, preferred_element_type=F32)


def direction_constants(slots):
    theta = np.arange(ND) * (2.0 * math.pi / ND)
    cosine, sine = np.cos(theta), np.sin(theta)
    table = np.zeros((2, slots, slots, LANES), np.float32)
    for slot in range(slots):
        for half in range(2):
            table[0, slot, slot, half * ND : (half + 1) * ND] = -cosine
            table[1, slot, slot, half * ND : (half + 1) * ND] = -sine
    table = table.reshape(2 * slots, slots * LANES)
    high = table.astype(ml_dtypes.bfloat16)
    low = (table - high.astype(np.float32)).astype(ml_dtypes.bfloat16)
    rows = np.stack([np.tile(cosine, 2), np.tile(sine, 2)]).astype(np.float32)
    facing = np.broadcast_to(rows[:, :, None], (2, PAIR, LANES))
    return np.concatenate([high, low, high], 0), np.ascontiguousarray(facing)


def vmem(shape, dtype=F32):
    return pltpu.VMEM(shape, dtype)


def in_hbm(*arrays):
    return [pltpu.with_memory_space_constraint(array, pltpu.HBM) for array in arrays]


def start_all(sources, targets, sems):
    copies = [
        pltpu.make_async_copy(source, target, sems.at[number])
        for number, (source, target) in enumerate(zip(sources, targets))
    ]
    for copy in copies:
        copy.start()
    return copies


def pick_kernel(
    lists_hbm, spec_hbm, spec_ref, first_ref, second_ref, lists_ref, chosen, sems, small_sems
):
    points = spec_ref.shape[1]
    chunks = sems.shape[0]
    width = points // chunks
    copies = []
    for chunk in range(chunks):
        columns = pl.ds(chunk * width, width)
        copies.append(
            pltpu.make_async_copy(
                spec_hbm.at[:, columns], spec_ref.at[:, columns], sems.at[chunk]
            )
        )
    (lists_copy,) = start_all([lists_hbm], [lists_ref], small_sems)
    for copy in copies:
        copy.start()
    lists_copy.wait()
    count = first_ref.shape[1]
    odd = lax.axis_index("wave") % 2
    lists = jnp.concatenate([lists_ref[odd], lists_ref[1 - odd]], 1)
    for start in range(0, points, LANES):
        ids = lax.broadcasted_iota(jnp.int32, (LANES, 2 * count), 0) + start
        chosen[start : start + LANES, :] = jnp.where(ids == lists, 1.0, 0.0).astype(BF)
    total = None
    for chunk in range(chunks):
        copies[chunk].wait()
        part = slice(chunk * width, (chunk + 1) * width)
        high, low = split2(spec_ref[:, part])
        found = dot(jnp.concatenate([high, low], 0), chosen[part, :])
        total = found if total is None else total + found
    bins = spec_ref.shape[0]
    total = total[:bins] + total[bins:]
    first_ref[...] = total[:, :count]
    second_ref[...] = total[:, count:]


def pick_halo(spectrum, lists):
    bins, points = spectrum.shape
    halo = jax.ShapeDtypeStruct((bins, lists.shape[-1]), F32)
    return pl.pallas_call(
        pick_kernel,
        in_specs=[ANY, ANY],
        out_specs=[VMEM] * 3,
        out_shape=[vmem((bins, points)), halo, halo],
        scratch_shapes=[
            pltpu.VMEM(lists.shape, jnp.int32),
            pltpu.VMEM((points, 2 * lists.shape[-1]), BF),
            pltpu.SemaphoreType.DMA((2,)),
            pltpu.SemaphoreType.DMA((1,)),
        ],
        compiler_params=params(8),
    )(*in_hbm(lists, spectrum))


def prepare_kernel(*refs):
    spec_ref, operands, blocks_hbm = refs[0], refs[1:11], refs[11]
    table, inflow, gain, index_ref, speed_rows, kernel_both, high_ref, low_ref = refs[12:20]
    scratch, (weights_ref, turn, sems, weights_sem) = refs[20:29], refs[29:]
    copies = start_all(operands, (*scratch, index_ref), sems)
    cells = high_ref.shape[1]
    mine = pl.ds(pl.multiple_of(lax.axis_index("grp") * cells, LANES), cells)
    weights_copy = pltpu.make_async_copy(blocks_hbm.at[:, :, mine], weights_ref, weights_sem)
    weights_copy.start()
    coef_ref, loss_ref, speed_ref, edge_ref, wind_ref, friction_ref = scratch[:6]
    weight_ref, facing_ref, kernel_ref = scratch[6:]
    bins, points = gain.shape
    groups = bins // PAIR
    slots = inflow.shape[0]
    filler = jnp.zeros((LANES - PAIR, LANES), F32)

    @pl.loop(0, points // LANES, unroll=8)
    def _(block):
        columns = pl.ds(pl.multiple_of(block * LANES, LANES), LANES)
        for group in range(groups):
            part = spec_ref[group * PAIR : (group + 1) * PAIR, columns]
            rows = pl.ds(block * (LANES * groups) + group, LANES, stride=groups)
            table[rows, :] = jnp.concatenate([part, filler], 0).T

    for copy in copies:
        copy.wait()
    index_ref[...] = index_ref[...] * groups
    kernel_high, kernel_low = split2(kernel_ref[...])
    kernel_both[...] = jnp.concatenate([kernel_high, kernel_low], 0)
    lower = lax.broadcasted_iota(jnp.int32, (PAIR, LANES), 0) < ND

    def per_bin(ref, group):
        return jnp.where(lower, ref[2 * group], ref[2 * group + 1])

    for group in range(groups):
        speed_rows[group * PAIR : (group + 1) * PAIR, :] = per_bin(speed_ref, group)
    coef = [per_bin(coef_ref, group) for group in range(groups)]
    loss = [per_bin(loss_ref, group) for group in range(groups)]
    turn[0] = jnp.cos(wind_ref[...])
    turn[1] = jnp.sin(wind_ref[...])

    @pl.loop(0, points // LANES, unroll=8)
    def _(block):
        base = pl.multiple_of(block * LANES, LANES)
        columns = pl.ds(base, LANES)
        edge_high, edge_low = split2(edge_ref[:, columns])
        left = jnp.concatenate([edge_high, edge_high, edge_low], 0)
        weights = lax.dot_general(
            left, weight_ref[...], (((0,), (0,)), ((), ())), preferred_element_type=F32
        )
        for slot in range(slots):
            factor = jnp.maximum(weights[:, slot * LANES : (slot + 1) * LANES], 0.0)
            inflow[slot, pl.ds(base, LANES), :] = factor
        row = pl.ds(block, 1)
        facing = facing_ref[0] * turn[0, row, :] + facing_ref[1] * turn[1, row, :]
        pushed = jnp.maximum(facing, 0.0) * friction_ref[row, :]
        for group in range(groups):
            gain[group * PAIR : (group + 1) * PAIR, columns] = jnp.exp(
                coef[group] * pushed - loss[group]
            )

    weights_copy.wait()
    count, block_rows, _ = weights_ref.shape

    @pl.loop(0, count, unroll=8)
    def _(block):
        high, low = split2(weights_ref[block])
        rows = pl.ds(pl.multiple_of(block * block_rows, block_rows), block_rows)
        high_ref[rows, :] = high
        low_ref[rows, :] = low


def prepare(spectrum, coef, loss, speed, edges, wind, friction, kernel, index, blocks, rows):
    bins, points = spectrum.shape
    slots = edges.shape[0] // 2
    weight, facing = direction_constants(slots)
    shape = (points // LANES, LANES)
    operands = [edges, wind.reshape(shape), friction.reshape(shape), weight, facing, kernel]
    operands = [jnp.asarray(operand) for operand in operands]
    count, block_rows, tile_cells = blocks.shape
    cells = tile_cells // lax.axis_size("grp")
    return pl.pallas_call(
        prepare_kernel,
        in_specs=[VMEM] + [ANY] * 11,
        out_specs=[VMEM] * 8,
        out_shape=[
            vmem((rows, LANES)),
            vmem((slots, points + 8, LANES)),
            vmem((bins, points)),
            vmem(index.shape, jnp.int32),
            vmem((bins, LANES)),
            vmem((2 * kernel.shape[0], bins), BF),
            vmem((count * block_rows, cells), BF),
            vmem((count * block_rows, cells), BF),
        ],
        scratch_shapes=[
            *[pltpu.SMEM(operand.shape, F32) for operand in (coef, loss, speed)],
            *[pltpu.VMEM(operand.shape, operand.dtype) for operand in operands],
            pltpu.VMEM((count, block_rows, cells), F32),
            pltpu.VMEM((2, *shape), F32),
            pltpu.SemaphoreType.DMA((10,)),
            pltpu.SemaphoreType.DMA(()),
        ],
        compiler_params=params(8),
    )(spectrum, *in_hbm(coef, loss, speed, *operands, index, blocks))


def advance_kernel(
    index_vmem,
    table_in,
    inflow,
    spec_ref,
    gain_ref,
    speed_rows,
    kernel_both,
    first_ref,
    second_ref,
    updated_ref,
    keep_ref,
    send_ref,
    table,
    index_ref,
    gathered,
    result,
    sems,
    index_sems,
    *,
    unroll,
):
    bins, points = spec_ref.shape
    groups = bins // PAIR
    slots = inflow.shape[0]
    halo = first_ref.shape[1]
    blocks = points // LANES
    depth = keep_ref.shape[0]
    filler = jnp.zeros((LANES - PAIR, LANES), F32)

    def fetch(block):
        return pltpu.make_async_copy(
            index_vmem.at[block], index_ref.at[block], index_sems.at[block]
        )

    @pl.loop(0, blocks)
    def _(block):
        fetch(block).start()

    right = lax.axis_index("wave") % 2
    for number, ref in ((1 - right, first_ref), (right, second_ref)):
        for group in range(groups):
            part = jnp.concatenate([ref[group * PAIR : (group + 1) * PAIR, :], filler], 0).T
            start = (points + number * halo) * groups + group
            table[pl.ds(start, halo, stride=groups), :] = part

    odd = lax.axis_index("grp") % 2
    width = result.shape[2]

    def copy_out(part, group):
        columns = pl.ds(pl.multiple_of(part * width, width), width)
        rows = pl.ds(group * PAIR, PAIR)
        return pltpu.make_async_copy(
            result.at[part, rows], updated_ref.at[rows, columns], sems.at[part, group]
        )

    def gather(block, start):
        fetch(block).wait()
        base = pl.multiple_of(block * LANES, LANES)

        @pl.loop(0, LANES // unroll)
        def _(chunk):
            first = pl.multiple_of(chunk * unroll, unroll)
            picks = [index_ref.at[block, slot, pl.ds(first, unroll)] for slot in range(slots)]
            for u in range(unroll):
                point = base + first + u
                own = table[pl.ds(point * groups, groups), :]
                terms = []
                for slot in range(slots):
                    upwind = table[pl.ds(picks[slot][u], groups), :]
                    factor = inflow[slot, pl.ds(point, groups, stride=0), :]
                    terms.append(factor * (upwind - own))
                while len(terms) > 1:
                    terms = [a + b for a, b in zip(terms[::2], terms[1::2])]
                gathered[pl.ds((start + first + u) * groups, groups), :] = terms[0]

    @pl.loop(0, points // width)
    def _(part):
        several = width // LANES

        @pl.loop(0, several)
        def _(step):
            gather(part * several + step, pl.multiple_of(step * LANES, LANES))

        for group in range(groups):
            rows = slice(group * PAIR, (group + 1) * PAIR)
            speed = speed_rows[rows, :]
            for step in range(several):
                inner = slice(step * LANES, (step + 1) * LANES)
                outer = pl.ds(pl.multiple_of(part * width + step * LANES, LANES), LANES)
                picked = gathered[pl.ds(step * LANES * groups + group, LANES, stride=groups), :]
                advected = spec_ref[rows, outer] + speed * picked.T[:PAIR]
                result[part, rows, inner] = advected * gain_ref[rows, outer]
            copy_out(part, group).start()
        high, low = split2(result[part])
        both = dot(kernel_both[...], high)
        stokes = both[:depth] + both[depth:] + dot(kernel_both[:depth, :], low)
        half_parts = points // width // 2
        local = pl.ds(pl.multiple_of(lax.rem(part, half_parts) * width, width), width)
        kept = (part >= half_parts) == (odd == 1)

        @pl.when(kept)
        def _():
            keep_ref[:, local] = stokes

        @pl.when(jnp.logical_not(kept))
        def _():
            send_ref[:, local] = stokes

    @pl.loop(0, points // width)
    def _(part):
        for group in range(groups):
            copy_out(part, group).wait()


def advance(index, table, inflow, spectrum, gain, speed_rows, kernel_both, first, second):
    bins, points = spectrum.shape
    groups = bins // PAIR
    blocks = points // LANES
    half = jax.ShapeDtypeStruct((kernel_both.shape[0] // 2, points // 2), F32)
    return pl.pallas_call(
        functools.partial(advance_kernel, unroll=UNROLL),
        in_specs=[VMEM] * 9,
        out_specs=[ANY, VMEM, VMEM, VMEM],
        out_shape=[jax.ShapeDtypeStruct((bins, points), F32), half, half, vmem(table.shape)],
        input_output_aliases={1: 3},
        scratch_shapes=[
            pltpu.SMEM(index.shape, jnp.int32),
            pltpu.VMEM((WIDTH * groups, LANES), F32),
            pltpu.VMEM((points // WIDTH, bins, WIDTH), F32),
            pltpu.SemaphoreType.DMA((points // WIDTH, groups)),
            pltpu.SemaphoreType.DMA((blocks,)),
        ],
        compiler_params=params(12),
    )(index, table, inflow, spectrum, gain, speed_rows, kernel_both, first, second)


def regrid_kernel(slot_ref, mine_ref, other_ref, high_ref, low_ref, out_ref, *, block_rows):
    depth, points = mine_ref.shape
    pairs = points // LANES
    odd = lax.axis_index("grp") % 2
    out_ref[...] = jnp.zeros(out_ref.shape, F32)
    lower = lax.broadcasted_iota(jnp.int32, (depth, LANES), 1) < block_rows
    for ref, half in ((mine_ref, odd), (other_ref, 1 - odd)):
        for pair in range(pairs):
            part = ref[:, pair * LANES : (pair + 1) * LANES]
            both = jnp.concatenate([jnp.where(lower, part, 0.0), jnp.where(lower, 0.0, part)], 0)
            high, low = split2(both)
            place = half * pairs + pair
            rows = pl.ds(pl.multiple_of(place * LANES, LANES), LANES)
            terms = (
                dot(high, high_ref[rows, :]) + dot(low, high_ref[rows, :]) + dot(high, low_ref[rows, :])
            )
            for side in range(2):
                slot = slot_ref[2 * place + side]
                out_ref[slot] = out_ref[slot] + terms[side * depth : (side + 1) * depth]


def regrid(slots, mine, other, high, low, count, block_rows):
    return pl.pallas_call(
        functools.partial(regrid_kernel, block_rows=block_rows),
        in_specs=[SMEM] + [VMEM] * 4,
        out_specs=VMEM,
        out_shape=jax.ShapeDtypeStruct((count, mine.shape[0], LANES), F32),
        compiler_params=params(4),
    )(slots, mine, other, high, low)


def swap(value, axis, bit):
    count = lax.axis_size(axis)
    return lax.ppermute(value, axis, [(i, i ^ bit) for i in range(count)])


def sum_over(keep, send, axis):
    mine = keep + swap(send, axis, 1)
    bit = 2
    while bit < lax.axis_size(axis):
        mine = mine + swap(mine, axis, bit)
        bit *= 2
    return mine, swap(mine, axis, 1)


def places(relative, bits):
    total = jnp.zeros_like(relative)
    for bit in bits:
        total = 2 * total + jnp.where((relative & bit) != 0, 1, 0)
    return total


def exchange(value, even_bit, odd_bit):
    waves, groups = lax.axis_size("wave"), lax.axis_size("grp")
    pairs = [
        (w * groups + g, (w ^ (odd_bit if g % 2 else even_bit)) * groups + g)
        for w in range(waves)
        for g in range(groups)
    ]
    return lax.ppermute(value, ("wave", "grp"), pairs)


def scatter_sum(parts, bits, other_bits):
    for bit, other in zip(bits, other_bits):
        half = parts.shape[0] // 2
        parts = parts[:half] + exchange(parts[half:], bit, other)
    return parts[0]


def swap_halo(first, second):
    count = lax.axis_size("wave")
    first = swap(first, "wave", 1)
    inner = [(i, i + 1 if i % 2 else i - 1) for i in range(1, count - 1)]
    return first, lax.ppermute(second, "wave", inner)


def body(
    spectrum,
    edge_vectors,
    neighbours,
    halo_lists,
    group_speed,
    input_coef,
    dissipation,
    friction,
    wind_dir,
    drift_kernel,
    block_tile,
    block_weights,
):
    n_wave = lax.axis_size("wave")
    bins, points = spectrum.shape
    groups = bins // PAIR
    slots = neighbours.shape[0]
    rows = (points + 2 * halo_lists.shape[-1]) * groups
    spectrum, first, second = pick_halo(spectrum, halo_lists)
    first, second = swap_halo(first, second)
    index = neighbours.reshape(slots, points // LANES, LANES).transpose(1, 0, 2)
    edges = edge_vectors.reshape(2 * slots, points)
    table, inflow, gain, index, speed_rows, kernel_both, high, low = prepare(
        spectrum,
        input_coef,
        dissipation,
        group_speed,
        edges,
        wind_dir,
        friction,
        drift_kernel,
        index,
        block_weights,
        rows,
    )
    updated, keep, send, _ = advance(
        index, table, inflow, spectrum, gain, speed_rows, kernel_both, first, second
    )
    mine, other = sum_over(keep, send, "grp")
    relative = (block_tile // TPW) ^ lax.axis_index("wave")
    tile = block_tile % TPW
    bits = [1 << b for b in range(n_wave.bit_length() - 1)]
    other_bits = bits[1::-1] + bits[2:]
    odd = lax.axis_index("grp") % 2 == 1
    place = jnp.where(odd, places(relative, other_bits), places(relative, bits))
    block_rows = block_weights.shape[1]
    parts = regrid(place * TPW + tile, mine, other, high, low, n_wave * TPW, block_rows)
    parts = parts.reshape(n_wave, TPW, *parts.shape[1:])
    drift = scatter_sum(parts, bits, other_bits)
    return updated, drift


def solution(mesh):
    in_specs = (
        P("grp", "wave"),
        P(None, None, "wave"),
        P(None, "wave"),
        P(None, "wave", None),
        P("grp"),
        P("grp"),
        P("grp"),
        P("wave"),
        P("wave"),
        P(None, "grp"),
        P("wave"),
        P("wave", None, None),
    )
    out_specs = (P("grp", "wave"), P("wave", None, "grp"))
    return jax.shard_map(body, mesh=mesh, in_specs=in_specs, out_specs=out_specs, check_vma=False)
```

```python
import functools
import math

import jax
import jax.numpy as jnp
import ml_dtypes
import numpy as np
from jax import lax
from jax.experimental import pallas as pl
from jax.experimental.pallas import tpu as pltpu
from jax.sharding import PartitionSpec as P

ND = 36
TPW = 4
LANES = 128
UNROLL = 128
WIDTH = 1024
PAIR = 2 * ND
BF = jnp.bfloat16
F32 = jnp.float32
VMEM = pl.BlockSpec(memory_space=pltpu.VMEM)
SMEM = pl.BlockSpec(memory_space=pltpu.SMEM)
ANY = pl.BlockSpec(memory_space=pl.ANY)


def params(mib):
    return pltpu.CompilerParams(vmem_limit_bytes=mib << 20)


def split2(x):
    high = x.astype(BF)
    return high, (x - high.astype(F32)).astype(BF)


def dot(a, b):
    return jnp.dot(a, b, preferred_element_type=F32)


def direction_constants(slots):
    theta = np.arange(ND) * (2.0 * math.pi / ND)
    cosine, sine = np.cos(theta), np.sin(theta)
    table = np.zeros((2, slots, slots, LANES), np.float32)
    for slot in range(slots):
        for half in range(2):
            table[0, slot, slot, half * ND : (half + 1) * ND] = -cosine
            table[1, slot, slot, half * ND : (half + 1) * ND] = -sine
    table = table.reshape(2 * slots, slots * LANES)
    high = table.astype(ml_dtypes.bfloat16)
    low = (table - high.astype(np.float32)).astype(ml_dtypes.bfloat16)
    rows = np.stack([np.tile(cosine, 2), np.tile(sine, 2)]).astype(np.float32)
    facing = np.broadcast_to(rows[:, :, None], (2, PAIR, LANES))
    return np.concatenate([high, low, high], 0), np.ascontiguousarray(facing)


def vmem(shape, dtype=F32):
    return pltpu.VMEM(shape, dtype)


def in_hbm(*arrays):
    return [pltpu.with_memory_space_constraint(array, pltpu.HBM) for array in arrays]


def start_all(sources, targets, sems):
    copies = [
        pltpu.make_async_copy(source, target, sems.at[number])
        for number, (source, target) in enumerate(zip(sources, targets))
    ]
    for copy in copies:
        copy.start()
    return copies


def pick_kernel(
    lists_hbm, spec_hbm, spec_ref, first_ref, second_ref, lists_ref, chosen, sems, small_sems
):
    points = spec_ref.shape[1]
    chunks = sems.shape[0]
    width = points // chunks
    copies = []
    for chunk in range(chunks):
        columns = pl.ds(chunk * width, width)
        copies.append(
            pltpu.make_async_copy(
                spec_hbm.at[:, columns], spec_ref.at[:, columns], sems.at[chunk]
            )
        )
    (lists_copy,) = start_all([lists_hbm], [lists_ref], small_sems)
    for copy in copies:
        copy.start()
    lists_copy.wait()
    count = first_ref.shape[1]
    odd = lax.axis_index("wave") % 2
    lists = jnp.concatenate([lists_ref[odd], lists_ref[1 - odd]], 1)
    for start in range(0, points, LANES):
        ids = lax.broadcasted_iota(jnp.int32, (LANES, 2 * count), 0) + start
        chosen[start : start + LANES, :] = jnp.where(ids == lists, 1.0, 0.0).astype(BF)
    total = None
    for chunk in range(chunks):
        copies[chunk].wait()
        part = slice(chunk * width, (chunk + 1) * width)
        high, low = split2(spec_ref[:, part])
        found = dot(jnp.concatenate([high, low], 0), chosen[part, :])
        total = found if total is None else total + found
    bins = spec_ref.shape[0]
    total = total[:bins] + total[bins:]
    first_ref[...] = total[:, :count]
    second_ref[...] = total[:, count:]


def pick_halo(spectrum, lists):
    bins, points = spectrum.shape
    halo = jax.ShapeDtypeStruct((bins, lists.shape[-1]), F32)
    return pl.pallas_call(
        pick_kernel,
        in_specs=[ANY, ANY],
        out_specs=[VMEM] * 3,
        out_shape=[vmem((bins, points)), halo, halo],
        scratch_shapes=[
            pltpu.VMEM(lists.shape, jnp.int32),
            pltpu.VMEM((points, 2 * lists.shape[-1]), BF),
            pltpu.SemaphoreType.DMA((2,)),
            pltpu.SemaphoreType.DMA((1,)),
        ],
        compiler_params=params(8),
    )(*in_hbm(lists, spectrum))


def prepare_kernel(*refs):
    spec_ref, operands, blocks_hbm = refs[0], refs[1:11], refs[11]
    table, inflow, gain, index_out, speed_rows, kernel_both, high_ref, low_ref = refs[12:20]
    scratch, (index_ref, weights_ref, turn, sems, weights_sem, index_sem) = refs[20:29], refs[29:]
    copies = start_all(operands, (*scratch, index_ref), sems)
    cells = high_ref.shape[1]
    mine = pl.ds(pl.multiple_of(lax.axis_index("grp") * cells, LANES), cells)
    weights_copy = pltpu.make_async_copy(blocks_hbm.at[:, :, mine], weights_ref, weights_sem)
    weights_copy.start()
    coef_ref, loss_ref, speed_ref, edge_ref, wind_ref, friction_ref = scratch[:6]
    weight_ref, facing_ref, kernel_ref = scratch[6:]
    bins, points = gain.shape
    groups = bins // PAIR
    slots = inflow.shape[0]
    filler = jnp.zeros((LANES - PAIR, LANES), F32)

    @pl.loop(0, points // LANES, unroll=8)
    def _(block):
        columns = pl.ds(pl.multiple_of(block * LANES, LANES), LANES)
        for group in range(groups):
            part = spec_ref[group * PAIR : (group + 1) * PAIR, columns]
            rows = pl.ds(block * (LANES * groups) + group, LANES, stride=groups)
            table[rows, :] = jnp.concatenate([part, filler], 0).T

    for copy in copies:
        copy.wait()
    index_ref[...] = index_ref[...] * groups
    index_copy = pltpu.make_async_copy(index_ref, index_out, index_sem)
    index_copy.start()
    kernel_high, kernel_low = split2(kernel_ref[...])
    kernel_both[...] = jnp.concatenate([kernel_high, kernel_low], 0)
    lower = lax.broadcasted_iota(jnp.int32, (PAIR, LANES), 0) < ND

    def per_bin(ref, group):
        return jnp.where(lower, ref[2 * group], ref[2 * group + 1])

    for group in range(groups):
        speed_rows[group * PAIR : (group + 1) * PAIR, :] = per_bin(speed_ref, group)
    coef = [per_bin(coef_ref, group) for group in range(groups)]
    loss = [per_bin(loss_ref, group) for group in range(groups)]
    turn[0] = jnp.cos(wind_ref[...])
    turn[1] = jnp.sin(wind_ref[...])

    @pl.loop(0, points // LANES, unroll=8)
    def _(block):
        base = pl.multiple_of(block * LANES, LANES)
        columns = pl.ds(base, LANES)
        edge_high, edge_low = split2(edge_ref[:, columns])
        left = jnp.concatenate([edge_high, edge_high, edge_low], 0)
        weights = lax.dot_general(
            left, weight_ref[...], (((0,), (0,)), ((), ())), preferred_element_type=F32
        )
        for slot in range(slots):
            factor = jnp.maximum(weights[:, slot * LANES : (slot + 1) * LANES], 0.0)
            inflow[slot, pl.ds(base, LANES), :] = factor
        row = pl.ds(block, 1)
        facing = facing_ref[0] * turn[0, row, :] + facing_ref[1] * turn[1, row, :]
        pushed = jnp.maximum(facing, 0.0) * friction_ref[row, :]
        for group in range(groups):
            gain[group * PAIR : (group + 1) * PAIR, columns] = jnp.exp(
                coef[group] * pushed - loss[group]
            )

    weights_copy.wait()
    count, block_rows, _ = weights_ref.shape

    @pl.loop(0, count, unroll=8)
    def _(block):
        high, low = split2(weights_ref[block])
        rows = pl.ds(pl.multiple_of(block * block_rows, block_rows), block_rows)
        high_ref[rows, :] = high
        low_ref[rows, :] = low

    index_copy.wait()


def prepare(spectrum, coef, loss, speed, edges, wind, friction, kernel, index, blocks, rows):
    bins, points = spectrum.shape
    slots = edges.shape[0] // 2
    weight, facing = direction_constants(slots)
    shape = (points // LANES, LANES)
    operands = [edges, wind.reshape(shape), friction.reshape(shape), weight, facing, kernel]
    operands = [jnp.asarray(operand) for operand in operands]
    count, block_rows, tile_cells = blocks.shape
    cells = tile_cells // lax.axis_size("grp")
    return pl.pallas_call(
        prepare_kernel,
        in_specs=[VMEM] + [ANY] * 11,
        out_specs=[VMEM] * 3 + [SMEM] + [VMEM] * 4,
        out_shape=[
            vmem((rows, LANES)),
            vmem((slots, points + 8, LANES)),
            vmem((bins, points)),
            pltpu.SMEM(index.shape, jnp.int32),
            vmem((bins, LANES)),
            vmem((2 * kernel.shape[0], bins), BF),
            vmem((count * block_rows, cells), BF),
            vmem((count * block_rows, cells), BF),
        ],
        scratch_shapes=[
            *[pltpu.SMEM(operand.shape, F32) for operand in (coef, loss, speed)],
            *[pltpu.VMEM(operand.shape, operand.dtype) for operand in operands],
            pltpu.VMEM(index.shape, jnp.int32),
            pltpu.VMEM((count, block_rows, cells), F32),
            pltpu.VMEM((2, *shape), F32),
            pltpu.SemaphoreType.DMA((10,)),
            pltpu.SemaphoreType.DMA(()),
            pltpu.SemaphoreType.DMA(()),
        ],
        compiler_params=params(8),
    )(spectrum, *in_hbm(coef, loss, speed, *operands, index, blocks))


def advance_kernel(
    index_ref,
    table_in,
    inflow,
    spec_ref,
    gain_ref,
    speed_rows,
    kernel_both,
    first_ref,
    second_ref,
    updated_ref,
    keep_ref,
    send_ref,
    table,
    gathered,
    result,
    sems,
    *,
    unroll,
):
    bins, points = spec_ref.shape
    groups = bins // PAIR
    slots = inflow.shape[0]
    halo = first_ref.shape[1]
    blocks = points // LANES
    depth = keep_ref.shape[0]
    filler = jnp.zeros((LANES - PAIR, LANES), F32)

    right = lax.axis_index("wave") % 2
    for number, ref in ((1 - right, first_ref), (right, second_ref)):
        for group in range(groups):
            part = jnp.concatenate([ref[group * PAIR : (group + 1) * PAIR, :], filler], 0).T
            start = (points + number * halo) * groups + group
            table[pl.ds(start, halo, stride=groups), :] = part

    odd = lax.axis_index("grp") % 2
    width = result.shape[2]

    def copy_out(part, group):
        columns = pl.ds(pl.multiple_of(part * width, width), width)
        rows = pl.ds(group * PAIR, PAIR)
        return pltpu.make_async_copy(
            result.at[part, rows], updated_ref.at[rows, columns], sems.at[part, group]
        )

    def gather(block, start):
        base = pl.multiple_of(block * LANES, LANES)

        @pl.loop(0, LANES // unroll)
        def _(chunk):
            first = pl.multiple_of(chunk * unroll, unroll)
            picks = [index_ref.at[block, slot, pl.ds(first, unroll)] for slot in range(slots)]
            for u in range(unroll):
                point = base + first + u
                own = table[pl.ds(point * groups, groups), :]
                terms = []
                for slot in range(slots):
                    upwind = table[pl.ds(picks[slot][u], groups), :]
                    factor = inflow[slot, pl.ds(point, groups, stride=0), :]
                    terms.append(factor * (upwind - own))
                while len(terms) > 1:
                    terms = [a + b for a, b in zip(terms[::2], terms[1::2])]
                gathered[pl.ds((start + first + u) * groups, groups), :] = terms[0]

    @pl.loop(0, points // width)
    def _(part):
        several = width // LANES

        @pl.loop(0, several)
        def _(step):
            gather(part * several + step, pl.multiple_of(step * LANES, LANES))

        for group in range(groups):
            rows = slice(group * PAIR, (group + 1) * PAIR)
            speed = speed_rows[rows, :]
            for step in range(several):
                inner = slice(step * LANES, (step + 1) * LANES)
                outer = pl.ds(pl.multiple_of(part * width + step * LANES, LANES), LANES)
                picked = gathered[pl.ds(step * LANES * groups + group, LANES, stride=groups), :]
                advected = spec_ref[rows, outer] + speed * picked.T[:PAIR]
                result[part, rows, inner] = advected * gain_ref[rows, outer]
            copy_out(part, group).start()
        high, low = split2(result[part])
        both = dot(kernel_both[...], high)
        stokes = both[:depth] + both[depth:] + dot(kernel_both[:depth, :], low)
        half_parts = points // width // 2
        local = pl.ds(pl.multiple_of(lax.rem(part, half_parts) * width, width), width)
        kept = (part >= half_parts) == (odd == 1)

        @pl.when(kept)
        def _():
            keep_ref[:, local] = stokes

        @pl.when(jnp.logical_not(kept))
        def _():
            send_ref[:, local] = stokes

    @pl.loop(0, points // width)
    def _(part):
        for group in range(groups):
            copy_out(part, group).wait()


def advance(index, table, inflow, spectrum, gain, speed_rows, kernel_both, first, second):
    bins, points = spectrum.shape
    groups = bins // PAIR
    blocks = points // LANES
    half = jax.ShapeDtypeStruct((kernel_both.shape[0] // 2, points // 2), F32)
    return pl.pallas_call(
        functools.partial(advance_kernel, unroll=UNROLL),
        in_specs=[SMEM] + [VMEM] * 8,
        out_specs=[ANY, VMEM, VMEM, VMEM],
        out_shape=[jax.ShapeDtypeStruct((bins, points), F32), half, half, vmem(table.shape)],
        input_output_aliases={1: 3},
        scratch_shapes=[
            pltpu.VMEM((WIDTH * groups, LANES), F32),
            pltpu.VMEM((points // WIDTH, bins, WIDTH), F32),
            pltpu.SemaphoreType.DMA((points // WIDTH, groups)),
        ],
        compiler_params=params(12),
    )(index, table, inflow, spectrum, gain, speed_rows, kernel_both, first, second)


def regrid_kernel(slot_ref, mine_ref, other_ref, high_ref, low_ref, out_ref, *, block_rows):
    depth, points = mine_ref.shape
    pairs = points // LANES
    odd = lax.axis_index("grp") % 2
    out_ref[...] = jnp.zeros(out_ref.shape, F32)
    lower = lax.broadcasted_iota(jnp.int32, (depth, LANES), 1) < block_rows
    for ref, half in ((mine_ref, odd), (other_ref, 1 - odd)):
        for pair in range(pairs):
            part = ref[:, pair * LANES : (pair + 1) * LANES]
            both = jnp.concatenate([jnp.where(lower, part, 0.0), jnp.where(lower, 0.0, part)], 0)
            high, low = split2(both)
            place = half * pairs + pair
            rows = pl.ds(pl.multiple_of(place * LANES, LANES), LANES)
            terms = (
                dot(high, high_ref[rows, :]) + dot(low, high_ref[rows, :]) + dot(high, low_ref[rows, :])
            )
            for side in range(2):
                slot = slot_ref[2 * place + side]
                out_ref[slot] = out_ref[slot] + terms[side * depth : (side + 1) * depth]


def regrid(slots, mine, other, high, low, count, block_rows):
    return pl.pallas_call(
        functools.partial(regrid_kernel, block_rows=block_rows),
        in_specs=[SMEM] + [VMEM] * 4,
        out_specs=VMEM,
        out_shape=jax.ShapeDtypeStruct((count, mine.shape[0], LANES), F32),
        compiler_params=params(4),
    )(slots, mine, other, high, low)


def swap(value, axis, bit):
    count = lax.axis_size(axis)
    return lax.ppermute(value, axis, [(i, i ^ bit) for i in range(count)])


def sum_over(keep, send, axis):
    mine = keep + swap(send, axis, 1)
    bit = 2
    while bit < lax.axis_size(axis):
        mine = mine + swap(mine, axis, bit)
        bit *= 2
    return mine, swap(mine, axis, 1)


def places(relative, bits):
    total = jnp.zeros_like(relative)
    for bit in bits:
        total = 2 * total + jnp.where((relative & bit) != 0, 1, 0)
    return total


def exchange(value, even_bit, odd_bit):
    waves, groups = lax.axis_size("wave"), lax.axis_size("grp")
    pairs = [
        (w * groups + g, (w ^ (odd_bit if g % 2 else even_bit)) * groups + g)
        for w in range(waves)
        for g in range(groups)
    ]
    return lax.ppermute(value, ("wave", "grp"), pairs)


def scatter_sum(parts, bits, other_bits):
    for bit, other in zip(bits, other_bits):
        half = parts.shape[0] // 2
        parts = parts[:half] + exchange(parts[half:], bit, other)
    return parts[0]


def swap_halo(first, second):
    count = lax.axis_size("wave")
    first = swap(first, "wave", 1)
    inner = [(i, i + 1 if i % 2 else i - 1) for i in range(1, count - 1)]
    return first, lax.ppermute(second, "wave", inner)


def body(
    spectrum,
    edge_vectors,
    neighbours,
    halo_lists,
    group_speed,
    input_coef,
    dissipation,
    friction,
    wind_dir,
    drift_kernel,
    block_tile,
    block_weights,
):
    n_wave = lax.axis_size("wave")
    bins, points = spectrum.shape
    groups = bins // PAIR
    slots = neighbours.shape[0]
    rows = (points + 2 * halo_lists.shape[-1]) * groups
    spectrum, first, second = pick_halo(spectrum, halo_lists)
    first, second = swap_halo(first, second)
    index = neighbours.reshape(slots, points // LANES, LANES).transpose(1, 0, 2)
    edges = edge_vectors.reshape(2 * slots, points)
    table, inflow, gain, index, speed_rows, kernel_both, high, low = prepare(
        spectrum,
        input_coef,
        dissipation,
        group_speed,
        edges,
        wind_dir,
        friction,
        drift_kernel,
        index,
        block_weights,
        rows,
    )
    updated, keep, send, _ = advance(
        index, table, inflow, spectrum, gain, speed_rows, kernel_both, first, second
    )
    mine, other = sum_over(keep, send, "grp")
    relative = (block_tile // TPW) ^ lax.axis_index("wave")
    tile = block_tile % TPW
    bits = [1 << b for b in range(n_wave.bit_length() - 1)]
    other_bits = bits[1::-1] + bits[2:]
    odd = lax.axis_index("grp") % 2 == 1
    place = jnp.where(odd, places(relative, other_bits), places(relative, bits))
    block_rows = block_weights.shape[1]
    parts = regrid(place * TPW + tile, mine, other, high, low, n_wave * TPW, block_rows)
    parts = parts.reshape(n_wave, TPW, *parts.shape[1:])
    drift = scatter_sum(parts, bits, other_bits)
    return updated, drift


def solution(mesh):
    in_specs = (
        P("grp", "wave"),
        P(None, None, "wave"),
        P(None, "wave"),
        P(None, "wave", None),
        P("grp"),
        P("grp"),
        P("grp"),
        P("wave"),
        P("wave"),
        P(None, "grp"),
        P("wave"),
        P("wave", None, None),
    )
    out_specs = (P("grp", "wave"), P("wave", None, "grp"))
    return jax.shard_map(body, mesh=mesh, in_specs=in_specs, out_specs=out_specs, check_vma=False)
```

```python
import functools
import math

import jax
import jax.numpy as jnp
import ml_dtypes
import numpy as np
from jax import lax
from jax.experimental import pallas as pl
from jax.experimental.pallas import tpu as pltpu
from jax.sharding import PartitionSpec as P

ND = 36
TPW = 4
LANES = 128
UNROLL = 128
WIDTH = 1024
PAIR = 2 * ND
BF = jnp.bfloat16
F32 = jnp.float32
VMEM = pl.BlockSpec(memory_space=pltpu.VMEM)
SMEM = pl.BlockSpec(memory_space=pltpu.SMEM)
ANY = pl.BlockSpec(memory_space=pl.ANY)


def params(mib):
    return pltpu.CompilerParams(vmem_limit_bytes=mib << 20)


def split2(x):
    high = x.astype(BF)
    return high, (x - high.astype(F32)).astype(BF)


def dot(a, b):
    return jnp.dot(a, b, preferred_element_type=F32)


def direction_constants(slots):
    theta = np.arange(ND) * (2.0 * math.pi / ND)
    cosine, sine = np.cos(theta), np.sin(theta)
    table = np.zeros((2, slots, slots, LANES), np.float32)
    for slot in range(slots):
        for half in range(2):
            table[0, slot, slot, half * ND : (half + 1) * ND] = -cosine
            table[1, slot, slot, half * ND : (half + 1) * ND] = -sine
    table = table.reshape(2 * slots, slots * LANES)
    high = table.astype(ml_dtypes.bfloat16)
    low = (table - high.astype(np.float32)).astype(ml_dtypes.bfloat16)
    rows = np.stack([np.tile(cosine, 2), np.tile(sine, 2)]).astype(np.float32)
    facing = np.broadcast_to(rows[:, :, None], (2, PAIR, LANES))
    return np.concatenate([high, low, high], 0), np.ascontiguousarray(facing)


def vmem(shape, dtype=F32):
    return pltpu.VMEM(shape, dtype)


def in_hbm(*arrays):
    return [pltpu.with_memory_space_constraint(array, pltpu.HBM) for array in arrays]


def start_all(sources, targets, sems):
    copies = [
        pltpu.make_async_copy(source, target, sems.at[number])
        for number, (source, target) in enumerate(zip(sources, targets))
    ]
    for copy in copies:
        copy.start()
    return copies


def pick_kernel(
    lists_hbm, spec_hbm, spec_ref, first_ref, second_ref, lists_ref, chosen, sems, small_sems
):
    points = spec_ref.shape[1]
    chunks = sems.shape[0]
    width = points // chunks
    copies = []
    for chunk in range(chunks):
        columns = pl.ds(chunk * width, width)
        copies.append(
            pltpu.make_async_copy(
                spec_hbm.at[:, columns], spec_ref.at[:, columns], sems.at[chunk]
            )
        )
    (lists_copy,) = start_all([lists_hbm], [lists_ref], small_sems)
    for copy in copies:
        copy.start()
    lists_copy.wait()
    count = first_ref.shape[1]
    odd = lax.axis_index("wave") % 2
    lists = jnp.concatenate([lists_ref[odd], lists_ref[1 - odd]], 1)
    for start in range(0, points, LANES):
        ids = lax.broadcasted_iota(jnp.int32, (LANES, 2 * count), 0) + start
        chosen[start : start + LANES, :] = jnp.where(ids == lists, 1.0, 0.0).astype(BF)
    total = None
    for chunk in range(chunks):
        copies[chunk].wait()
        part = slice(chunk * width, (chunk + 1) * width)
        high, low = split2(spec_ref[:, part])
        found = dot(jnp.concatenate([high, low], 0), chosen[part, :])
        total = found if total is None else total + found
    bins = spec_ref.shape[0]
    total = total[:bins] + total[bins:]
    first_ref[...] = total[:, :count]
    second_ref[...] = total[:, count:]


def pick_halo(spectrum, lists):
    bins, points = spectrum.shape
    halo = jax.ShapeDtypeStruct((bins, lists.shape[-1]), F32)
    return pl.pallas_call(
        pick_kernel,
        in_specs=[ANY, ANY],
        out_specs=[VMEM] * 3,
        out_shape=[vmem((bins, points)), halo, halo],
        scratch_shapes=[
            pltpu.VMEM(lists.shape, jnp.int32),
            pltpu.VMEM((points, 2 * lists.shape[-1]), BF),
            pltpu.SemaphoreType.DMA((2,)),
            pltpu.SemaphoreType.DMA((1,)),
        ],
        compiler_params=params(8),
    )(*in_hbm(lists, spectrum))


def places(relative, bits):
    total = 0
    for bit in bits:
        total = 2 * total + jnp.where((relative & bit) != 0, 1, 0)
    return total


def prepare_kernel(*refs, orders):
    spec_ref, operands, blocks_hbm, tile_hbm = refs[0], refs[1:11], refs[11], refs[12]
    table, inflow, gain, index_out, speed_rows, kernel_both, high_ref, low_ref, slot_ref = refs[13:22]
    scratch, (tile_ref, index_ref, weights_ref, turn, sems, weights_sem, index_sem) = (
        refs[22:31],
        refs[31:],
    )
    copies = start_all((*operands, tile_hbm), (*scratch, index_ref, tile_ref), sems)
    cells = high_ref.shape[1]
    mine = pl.ds(pl.multiple_of(lax.axis_index("grp") * cells, LANES), cells)
    weights_copy = pltpu.make_async_copy(blocks_hbm.at[:, :, mine], weights_ref, weights_sem)
    weights_copy.start()
    coef_ref, loss_ref, speed_ref, edge_ref, wind_ref, friction_ref = scratch[:6]
    weight_ref, facing_ref, kernel_ref = scratch[6:]
    bins, points = gain.shape
    groups = bins // PAIR
    slots = inflow.shape[0]
    filler = jnp.zeros((LANES - PAIR, LANES), F32)

    @pl.loop(0, points // LANES, unroll=8)
    def _(block):
        columns = pl.ds(pl.multiple_of(block * LANES, LANES), LANES)
        for group in range(groups):
            part = spec_ref[group * PAIR : (group + 1) * PAIR, columns]
            rows = pl.ds(block * (LANES * groups) + group, LANES, stride=groups)
            table[rows, :] = jnp.concatenate([part, filler], 0).T

    for copy in copies:
        copy.wait()
    index_ref[...] = index_ref[...] * groups
    index_copy = pltpu.make_async_copy(index_ref, index_out, index_sem)
    index_copy.start()
    wave = lax.axis_index("wave")
    odd = lax.axis_index("grp") % 2 == 1

    @pl.loop(0, tile_ref.shape[0])
    def _(block):
        tile = tile_ref[block]
        relative = lax.div(tile, TPW) ^ wave
        place = jnp.where(odd, places(relative, orders[1]), places(relative, orders[0]))
        slot_ref[block] = place * TPW + lax.rem(tile, TPW)

    kernel_high, kernel_low = split2(kernel_ref[...])
    kernel_both[...] = jnp.concatenate([kernel_high, kernel_low], 0)
    lower = lax.broadcasted_iota(jnp.int32, (PAIR, LANES), 0) < ND

    def per_bin(ref, group):
        return jnp.where(lower, ref[2 * group], ref[2 * group + 1])

    for group in range(groups):
        speed_rows[group * PAIR : (group + 1) * PAIR, :] = per_bin(speed_ref, group)
    coef = [per_bin(coef_ref, group) for group in range(groups)]
    loss = [per_bin(loss_ref, group) for group in range(groups)]
    turn[0] = jnp.cos(wind_ref[...])
    turn[1] = jnp.sin(wind_ref[...])

    @pl.loop(0, points // LANES, unroll=8)
    def _(block):
        base = pl.multiple_of(block * LANES, LANES)
        columns = pl.ds(base, LANES)
        edge_high, edge_low = split2(edge_ref[:, columns])
        left = jnp.concatenate([edge_high, edge_high, edge_low], 0)
        weights = lax.dot_general(
            left, weight_ref[...], (((0,), (0,)), ((), ())), preferred_element_type=F32
        )
        for slot in range(slots):
            factor = jnp.maximum(weights[:, slot * LANES : (slot + 1) * LANES], 0.0)
            inflow[slot, pl.ds(base, LANES), :] = factor
        row = pl.ds(block, 1)
        facing = facing_ref[0] * turn[0, row, :] + facing_ref[1] * turn[1, row, :]
        pushed = jnp.maximum(facing, 0.0) * friction_ref[row, :]
        for group in range(groups):
            gain[group * PAIR : (group + 1) * PAIR, columns] = jnp.exp(
                coef[group] * pushed - loss[group]
            )

    weights_copy.wait()
    count, block_rows, _ = weights_ref.shape

    @pl.loop(0, count, unroll=8)
    def _(block):
        high, low = split2(weights_ref[block])
        rows = pl.ds(pl.multiple_of(block * block_rows, block_rows), block_rows)
        high_ref[rows, :] = high
        low_ref[rows, :] = low

    index_copy.wait()


def prepare(
    spectrum, coef, loss, speed, edges, wind, friction, kernel, index, blocks, tiles, rows, orders
):
    bins, points = spectrum.shape
    slots = edges.shape[0] // 2
    weight, facing = direction_constants(slots)
    shape = (points // LANES, LANES)
    operands = [edges, wind.reshape(shape), friction.reshape(shape), weight, facing, kernel]
    operands = [jnp.asarray(operand) for operand in operands]
    count, block_rows, tile_cells = blocks.shape
    cells = tile_cells // lax.axis_size("grp")
    return pl.pallas_call(
        functools.partial(prepare_kernel, orders=orders),
        in_specs=[VMEM] + [ANY] * 12,
        out_specs=[VMEM] * 3 + [SMEM] + [VMEM] * 4 + [SMEM],
        out_shape=[
            vmem((rows, LANES)),
            vmem((slots, points + 8, LANES)),
            vmem((bins, points)),
            pltpu.SMEM(index.shape, jnp.int32),
            vmem((bins, LANES)),
            vmem((2 * kernel.shape[0], bins), BF),
            vmem((count * block_rows, cells), BF),
            vmem((count * block_rows, cells), BF),
            pltpu.SMEM(tiles.shape, jnp.int32),
        ],
        scratch_shapes=[
            *[pltpu.SMEM(operand.shape, F32) for operand in (coef, loss, speed)],
            *[pltpu.VMEM(operand.shape, operand.dtype) for operand in operands],
            pltpu.SMEM(tiles.shape, jnp.int32),
            pltpu.VMEM(index.shape, jnp.int32),
            pltpu.VMEM((count, block_rows, cells), F32),
            pltpu.VMEM((2, *shape), F32),
            pltpu.SemaphoreType.DMA((11,)),
            pltpu.SemaphoreType.DMA(()),
            pltpu.SemaphoreType.DMA(()),
        ],
        compiler_params=params(8),
    )(spectrum, *in_hbm(coef, loss, speed, *operands, index, blocks, tiles))


def advance_kernel(
    index_ref,
    table_in,
    inflow,
    spec_ref,
    gain_ref,
    speed_rows,
    kernel_both,
    first_ref,
    second_ref,
    updated_ref,
    keep_ref,
    send_ref,
    table,
    gathered,
    result,
    sems,
    *,
    unroll,
):
    bins, points = spec_ref.shape
    groups = bins // PAIR
    slots = inflow.shape[0]
    halo = first_ref.shape[1]
    blocks = points // LANES
    depth = keep_ref.shape[0]
    filler = jnp.zeros((LANES - PAIR, LANES), F32)

    right = lax.axis_index("wave") % 2
    for number, ref in ((1 - right, first_ref), (right, second_ref)):
        for group in range(groups):
            part = jnp.concatenate([ref[group * PAIR : (group + 1) * PAIR, :], filler], 0).T
            start = (points + number * halo) * groups + group
            table[pl.ds(start, halo, stride=groups), :] = part

    odd = lax.axis_index("grp") % 2
    width = result.shape[2]

    def copy_out(part, group):
        columns = pl.ds(pl.multiple_of(part * width, width), width)
        rows = pl.ds(group * PAIR, PAIR)
        return pltpu.make_async_copy(
            result.at[part, rows], updated_ref.at[rows, columns], sems.at[part, group]
        )

    def gather(block, start):
        base = pl.multiple_of(block * LANES, LANES)

        @pl.loop(0, LANES // unroll)
        def _(chunk):
            first = pl.multiple_of(chunk * unroll, unroll)
            picks = [index_ref.at[block, slot, pl.ds(first, unroll)] for slot in range(slots)]
            for u in range(unroll):
                point = base + first + u
                own = table[pl.ds(point * groups, groups), :]
                terms = []
                for slot in range(slots):
                    upwind = table[pl.ds(picks[slot][u], groups), :]
                    factor = inflow[slot, pl.ds(point, groups, stride=0), :]
                    terms.append(factor * (upwind - own))
                while len(terms) > 1:
                    terms = [a + b for a, b in zip(terms[::2], terms[1::2])]
                gathered[pl.ds((start + first + u) * groups, groups), :] = terms[0]

    @pl.loop(0, points // width)
    def _(part):
        several = width // LANES

        @pl.loop(0, several)
        def _(step):
            gather(part * several + step, pl.multiple_of(step * LANES, LANES))

        for group in range(groups):
            rows = slice(group * PAIR, (group + 1) * PAIR)
            speed = speed_rows[rows, :]
            for step in range(several):
                inner = slice(step * LANES, (step + 1) * LANES)
                outer = pl.ds(pl.multiple_of(part * width + step * LANES, LANES), LANES)
                picked = gathered[pl.ds(step * LANES * groups + group, LANES, stride=groups), :]
                advected = spec_ref[rows, outer] + speed * picked.T[:PAIR]
                result[part, rows, inner] = advected * gain_ref[rows, outer]
            copy_out(part, group).start()
        high, low = split2(result[part])
        both = dot(kernel_both[...], high)
        stokes = both[:depth] + both[depth:] + dot(kernel_both[:depth, :], low)
        half_parts = points // width // 2
        local = pl.ds(pl.multiple_of(lax.rem(part, half_parts) * width, width), width)
        kept = (part >= half_parts) == (odd == 1)

        @pl.when(kept)
        def _():
            keep_ref[:, local] = stokes

        @pl.when(jnp.logical_not(kept))
        def _():
            send_ref[:, local] = stokes

    @pl.loop(0, points // width)
    def _(part):
        for group in range(groups):
            copy_out(part, group).wait()


def advance(index, table, inflow, spectrum, gain, speed_rows, kernel_both, first, second):
    bins, points = spectrum.shape
    groups = bins // PAIR
    blocks = points // LANES
    half = jax.ShapeDtypeStruct((kernel_both.shape[0] // 2, points // 2), F32)
    return pl.pallas_call(
        functools.partial(advance_kernel, unroll=UNROLL),
        in_specs=[SMEM] + [VMEM] * 8,
        out_specs=[ANY, VMEM, VMEM, VMEM],
        out_shape=[jax.ShapeDtypeStruct((bins, points), F32), half, half, vmem(table.shape)],
        input_output_aliases={1: 3},
        scratch_shapes=[
            pltpu.VMEM((WIDTH * groups, LANES), F32),
            pltpu.VMEM((points // WIDTH, bins, WIDTH), F32),
            pltpu.SemaphoreType.DMA((points // WIDTH, groups)),
        ],
        compiler_params=params(12),
    )(index, table, inflow, spectrum, gain, speed_rows, kernel_both, first, second)


def regrid_kernel(slot_ref, high_ref, low_ref, stokes_ref, *refs, block_rows, own):
    out_ref = refs[-1]
    depth, points = stokes_ref.shape
    pairs = points // LANES
    odd = lax.axis_index("grp") % 2
    half = odd if own else 1 - odd
    if own:
        out_ref[...] = jnp.zeros(out_ref.shape, F32)
    lower = lax.broadcasted_iota(jnp.int32, (depth, LANES), 1) < block_rows
    for pair in range(pairs):
        part = stokes_ref[:, pair * LANES : (pair + 1) * LANES]
        both = jnp.concatenate([jnp.where(lower, part, 0.0), jnp.where(lower, 0.0, part)], 0)
        high, low = split2(both)
        place = half * pairs + pair
        rows = pl.ds(pl.multiple_of(place * LANES, LANES), LANES)
        terms = dot(high, high_ref[rows, :]) + dot(low, high_ref[rows, :]) + dot(high, low_ref[rows, :])
        for side in range(2):
            slot = slot_ref[2 * place + side]
            out_ref[slot] = out_ref[slot] + terms[side * depth : (side + 1) * depth]


def regrid(slots, mine, other, high, low, count, block_rows):
    total = []
    for stokes in (mine, other):
        total = [
            pl.pallas_call(
                functools.partial(regrid_kernel, block_rows=block_rows, own=not total),
                in_specs=[SMEM] + [VMEM] * (3 + len(total)),
                out_specs=VMEM,
                out_shape=jax.ShapeDtypeStruct((count, mine.shape[0], LANES), F32),
                input_output_aliases={4: 0} if total else {},
                compiler_params=params(4),
            )(slots, high, low, stokes, *total)
        ]
    return total[0]


def swap(value, axis, bit):
    count = lax.axis_size(axis)
    return lax.ppermute(value, axis, [(i, i ^ bit) for i in range(count)])


def sum_over(keep, send, axis):
    mine = keep + swap(send, axis, 1)
    bit = 2
    while bit < lax.axis_size(axis):
        mine = mine + swap(mine, axis, bit)
        bit *= 2
    return mine, swap(mine, axis, 1)


def exchange(value, even_bit, odd_bit):
    waves, groups = lax.axis_size("wave"), lax.axis_size("grp")
    pairs = [
        (w * groups + g, (w ^ (odd_bit if g % 2 else even_bit)) * groups + g)
        for w in range(waves)
        for g in range(groups)
    ]
    return lax.ppermute(value, ("wave", "grp"), pairs)


def scatter_sum(parts, bits, other_bits):
    for bit, other in zip(bits, other_bits):
        half = parts.shape[0] // 2
        parts = parts[:half] + exchange(parts[half:], bit, other)
    return parts[0]


def swap_halo(first, second):
    count = lax.axis_size("wave")
    first = swap(first, "wave", 1)
    inner = [(i, i + 1 if i % 2 else i - 1) for i in range(1, count - 1)]
    return first, lax.ppermute(second, "wave", inner)


def body(
    spectrum,
    edge_vectors,
    neighbours,
    halo_lists,
    group_speed,
    input_coef,
    dissipation,
    friction,
    wind_dir,
    drift_kernel,
    block_tile,
    block_weights,
):
    n_wave = lax.axis_size("wave")
    bins, points = spectrum.shape
    groups = bins // PAIR
    slots = neighbours.shape[0]
    rows = (points + 2 * halo_lists.shape[-1]) * groups
    bits = [1 << b for b in range(n_wave.bit_length() - 1)]
    other_bits = bits[1::-1] + bits[2:]
    spectrum, first, second = pick_halo(spectrum, halo_lists)
    first, second = swap_halo(first, second)
    index = neighbours.reshape(slots, points // LANES, LANES).transpose(1, 0, 2)
    edges = edge_vectors.reshape(2 * slots, points)
    table, inflow, gain, index, speed_rows, kernel_both, high, low, slot = prepare(
        spectrum,
        input_coef,
        dissipation,
        group_speed,
        edges,
        wind_dir,
        friction,
        drift_kernel,
        index,
        block_weights,
        block_tile,
        rows,
        (bits, other_bits),
    )
    updated, keep, send, _ = advance(
        index, table, inflow, spectrum, gain, speed_rows, kernel_both, first, second
    )
    mine, other = sum_over(keep, send, "grp")
    block_rows = block_weights.shape[1]
    parts = regrid(slot, mine, other, high, low, n_wave * TPW, block_rows)
    parts = parts.reshape(n_wave, TPW, *parts.shape[1:])
    drift = scatter_sum(parts, bits, other_bits)
    return updated, drift


def solution(mesh):
    in_specs = (
        P("grp", "wave"),
        P(None, None, "wave"),
        P(None, "wave"),
        P(None, "wave", None),
        P("grp"),
        P("grp"),
        P("grp"),
        P("wave"),
        P("wave"),
        P(None, "grp"),
        P("wave"),
        P("wave", None, None),
    )
    out_specs = (P("grp", "wave"), P("wave", None, "grp"))
    return jax.shard_map(body, mesh=mesh, in_specs=in_specs, out_specs=out_specs, check_vma=False)
```

```python
import functools
import math

import jax
import jax.numpy as jnp
import ml_dtypes
import numpy as np
from jax import lax
from jax.experimental import pallas as pl
from jax.experimental.pallas import tpu as pltpu
from jax.sharding import PartitionSpec as P

ND = 36
TPW = 4
LANES = 128
UNROLL = 128
WIDTH = 1024
PAIR = 2 * ND
BF = jnp.bfloat16
F32 = jnp.float32
VMEM = pl.BlockSpec(memory_space=pltpu.VMEM)
SMEM = pl.BlockSpec(memory_space=pltpu.SMEM)
ANY = pl.BlockSpec(memory_space=pl.ANY)


def params(mib):
    return pltpu.CompilerParams(vmem_limit_bytes=mib << 20)


def split2(x):
    high = x.astype(BF)
    return high, (x - high.astype(F32)).astype(BF)


def dot(a, b):
    return jnp.dot(a, b, preferred_element_type=F32)


def direction_constants(slots):
    theta = np.arange(ND) * (2.0 * math.pi / ND)
    cosine, sine = np.cos(theta), np.sin(theta)
    table = np.zeros((2, slots, slots, LANES), np.float32)
    for slot in range(slots):
        for half in range(2):
            table[0, slot, slot, half * ND : (half + 1) * ND] = -cosine
            table[1, slot, slot, half * ND : (half + 1) * ND] = -sine
    table = table.reshape(2 * slots, slots * LANES)
    high = table.astype(ml_dtypes.bfloat16)
    low = (table - high.astype(np.float32)).astype(ml_dtypes.bfloat16)
    rows = np.stack([np.tile(cosine, 2), np.tile(sine, 2)]).astype(np.float32)
    facing = np.broadcast_to(rows[:, :, None], (2, PAIR, LANES))
    return np.concatenate([high, low, high], 0), np.ascontiguousarray(facing)


def vmem(shape, dtype=F32):
    return pltpu.VMEM(shape, dtype)


def in_hbm(*arrays):
    return [pltpu.with_memory_space_constraint(array, pltpu.HBM) for array in arrays]


def start_all(sources, targets, sems):
    copies = [
        pltpu.make_async_copy(source, target, sems.at[number])
        for number, (source, target) in enumerate(zip(sources, targets))
    ]
    for copy in copies:
        copy.start()
    return copies


def pick_kernel(
    lists_hbm, spec_hbm, spec_ref, first_ref, second_ref, lists_ref, chosen, sems, small_sems
):
    points = spec_ref.shape[1]
    chunks = sems.shape[0]
    width = points // chunks
    copies = []
    for chunk in range(chunks):
        columns = pl.ds(chunk * width, width)
        copies.append(
            pltpu.make_async_copy(
                spec_hbm.at[:, columns], spec_ref.at[:, columns], sems.at[chunk]
            )
        )
    (lists_copy,) = start_all([lists_hbm], [lists_ref], small_sems)
    for copy in copies:
        copy.start()
    lists_copy.wait()
    count = first_ref.shape[1]
    odd = lax.axis_index("wave") % 2
    lists = jnp.concatenate([lists_ref[odd], lists_ref[1 - odd]], 1)
    for start in range(0, points, LANES):
        ids = lax.broadcasted_iota(jnp.int32, (LANES, 2 * count), 0) + start
        chosen[start : start + LANES, :] = jnp.where(ids == lists, 1.0, 0.0).astype(BF)
    total = None
    for chunk in range(chunks):
        copies[chunk].wait()
        part = slice(chunk * width, (chunk + 1) * width)
        high, low = split2(spec_ref[:, part])
        found = dot(jnp.concatenate([high, low], 0), chosen[part, :])
        total = found if total is None else total + found
    bins = spec_ref.shape[0]
    total = total[:bins] + total[bins:]
    first_ref[...] = total[:, :count]
    second_ref[...] = total[:, count:]


def pick_halo(spectrum, lists):
    bins, points = spectrum.shape
    halo = jax.ShapeDtypeStruct((bins, lists.shape[-1]), F32)
    return pl.pallas_call(
        pick_kernel,
        in_specs=[ANY, ANY],
        out_specs=[VMEM] * 3,
        out_shape=[vmem((bins, points)), halo, halo],
        scratch_shapes=[
            pltpu.VMEM(lists.shape, jnp.int32),
            pltpu.VMEM((points, 2 * lists.shape[-1]), BF),
            pltpu.SemaphoreType.DMA((2,)),
            pltpu.SemaphoreType.DMA((1,)),
        ],
        compiler_params=params(8),
    )(*in_hbm(lists, spectrum))


def places(relative, bits):
    total = 0
    for bit in bits:
        total = 2 * total + jnp.where((relative & bit) != 0, 1, 0)
    return total


def prepare_kernel(*refs, orders):
    spec_ref, operands, blocks_hbm, tile_hbm = refs[0], refs[1:11], refs[11], refs[12]
    table, inflow, gain, index_out, speed_rows, kernel_both, high_ref, low_ref, slot_ref = refs[13:22]
    scratch, (tile_ref, index_ref, weights_ref, turn, sems, weights_sem, index_sem) = (
        refs[22:31],
        refs[31:],
    )
    copies = start_all((*operands, tile_hbm), (*scratch, index_ref, tile_ref), sems)
    cells = high_ref.shape[1]
    mine = pl.ds(pl.multiple_of(lax.axis_index("grp") * cells, LANES), cells)
    weights_copy = pltpu.make_async_copy(blocks_hbm.at[:, :, mine], weights_ref, weights_sem)
    weights_copy.start()
    coef_ref, loss_ref, speed_ref, edge_ref, wind_ref, friction_ref = scratch[:6]
    weight_ref, facing_ref, kernel_ref = scratch[6:]
    bins, points = gain.shape
    groups = bins // PAIR
    slots = inflow.shape[0]
    filler = jnp.zeros((LANES - PAIR, LANES), F32)

    @pl.loop(0, points // LANES, unroll=4)
    def _(block):
        columns = pl.ds(pl.multiple_of(block * LANES, LANES), LANES)
        for group in range(groups):
            part = spec_ref[group * PAIR : (group + 1) * PAIR, columns]
            rows = pl.ds(block * (LANES * groups) + group, LANES, stride=groups)
            table[rows, :] = jnp.concatenate([part, filler], 0).T

    for copy in copies:
        copy.wait()
    index_ref[...] = index_ref[...] * groups
    index_copy = pltpu.make_async_copy(index_ref, index_out, index_sem)
    index_copy.start()
    wave = lax.axis_index("wave")
    odd = lax.axis_index("grp") % 2 == 1

    @pl.loop(0, tile_ref.shape[0])
    def _(block):
        tile = tile_ref[block]
        relative = lax.div(tile, TPW) ^ wave
        place = jnp.where(odd, places(relative, orders[1]), places(relative, orders[0]))
        slot_ref[block] = place * TPW + lax.rem(tile, TPW)

    kernel_high, kernel_low = split2(kernel_ref[...])
    kernel_both[...] = jnp.concatenate([kernel_high, kernel_low], 0)
    lower = lax.broadcasted_iota(jnp.int32, (PAIR, LANES), 0) < ND

    def per_bin(ref, group):
        return jnp.where(lower, ref[2 * group], ref[2 * group + 1])

    for group in range(groups):
        speed_rows[group * PAIR : (group + 1) * PAIR, :] = per_bin(speed_ref, group)
    coef = [per_bin(coef_ref, group) for group in range(groups)]
    loss = [per_bin(loss_ref, group) for group in range(groups)]
    turn[0] = jnp.cos(wind_ref[...])
    turn[1] = jnp.sin(wind_ref[...])

    @pl.loop(0, points // LANES, unroll=4)
    def _(block):
        base = pl.multiple_of(block * LANES, LANES)
        columns = pl.ds(base, LANES)
        edge_high, edge_low = split2(edge_ref[:, columns])
        left = jnp.concatenate([edge_high, edge_high, edge_low], 0)
        weights = lax.dot_general(
            left, weight_ref[...], (((0,), (0,)), ((), ())), preferred_element_type=F32
        )
        for slot in range(slots):
            factor = jnp.maximum(weights[:, slot * LANES : (slot + 1) * LANES], 0.0)
            inflow[slot, pl.ds(base, LANES), :] = factor
        row = pl.ds(block, 1)
        facing = facing_ref[0] * turn[0, row, :] + facing_ref[1] * turn[1, row, :]
        pushed = jnp.maximum(facing, 0.0) * friction_ref[row, :]
        for group in range(groups):
            gain[group * PAIR : (group + 1) * PAIR, columns] = jnp.exp(
                coef[group] * pushed - loss[group]
            )

    weights_copy.wait()
    count, block_rows, _ = weights_ref.shape

    @pl.loop(0, count, unroll=8)
    def _(block):
        high, low = split2(weights_ref[block])
        rows = pl.ds(pl.multiple_of(block * block_rows, block_rows), block_rows)
        high_ref[rows, :] = high
        low_ref[rows, :] = low

    index_copy.wait()


def prepare(
    spectrum, coef, loss, speed, edges, wind, friction, kernel, index, blocks, tiles, rows, orders
):
    bins, points = spectrum.shape
    slots = edges.shape[0] // 2
    weight, facing = direction_constants(slots)
    shape = (points // LANES, LANES)
    operands = [edges, wind.reshape(shape), friction.reshape(shape), weight, facing, kernel]
    operands = [jnp.asarray(operand) for operand in operands]
    count, block_rows, tile_cells = blocks.shape
    cells = tile_cells // lax.axis_size("grp")
    return pl.pallas_call(
        functools.partial(prepare_kernel, orders=orders),
        in_specs=[VMEM] + [ANY] * 12,
        out_specs=[VMEM] * 3 + [SMEM] + [VMEM] * 4 + [SMEM],
        out_shape=[
            vmem((rows, LANES)),
            vmem((slots, points + 8, LANES)),
            vmem((bins, points)),
            pltpu.SMEM(index.shape, jnp.int32),
            vmem((bins, LANES)),
            vmem((2 * kernel.shape[0], bins), BF),
            vmem((count * block_rows, cells), BF),
            vmem((count * block_rows, cells), BF),
            pltpu.SMEM(tiles.shape, jnp.int32),
        ],
        scratch_shapes=[
            *[pltpu.SMEM(operand.shape, F32) for operand in (coef, loss, speed)],
            *[pltpu.VMEM(operand.shape, operand.dtype) for operand in operands],
            pltpu.SMEM(tiles.shape, jnp.int32),
            pltpu.VMEM(index.shape, jnp.int32),
            pltpu.VMEM((count, block_rows, cells), F32),
            pltpu.VMEM((2, *shape), F32),
            pltpu.SemaphoreType.DMA((11,)),
            pltpu.SemaphoreType.DMA(()),
            pltpu.SemaphoreType.DMA(()),
        ],
        compiler_params=params(8),
    )(spectrum, *in_hbm(coef, loss, speed, *operands, index, blocks, tiles))


def advance_kernel(
    index_ref,
    table_in,
    inflow,
    spec_ref,
    gain_ref,
    speed_rows,
    kernel_both,
    first_ref,
    second_ref,
    updated_ref,
    keep_ref,
    send_ref,
    table,
    gathered,
    result,
    sems,
    *,
    unroll,
):
    bins, points = spec_ref.shape
    groups = bins // PAIR
    slots = inflow.shape[0]
    halo = first_ref.shape[1]
    blocks = points // LANES
    depth = keep_ref.shape[0]
    filler = jnp.zeros((LANES - PAIR, LANES), F32)

    right = lax.axis_index("wave") % 2
    for number, ref in ((1 - right, first_ref), (right, second_ref)):
        for group in range(groups):
            part = jnp.concatenate([ref[group * PAIR : (group + 1) * PAIR, :], filler], 0).T
            start = (points + number * halo) * groups + group
            table[pl.ds(start, halo, stride=groups), :] = part

    odd = lax.axis_index("grp") % 2
    width = result.shape[2]

    def copy_out(part, group):
        columns = pl.ds(pl.multiple_of(part * width, width), width)
        rows = pl.ds(group * PAIR, PAIR)
        return pltpu.make_async_copy(
            result.at[part, rows], updated_ref.at[rows, columns], sems.at[part, group]
        )

    def gather(block, start):
        base = pl.multiple_of(block * LANES, LANES)

        @pl.loop(0, LANES // unroll)
        def _(chunk):
            first = pl.multiple_of(chunk * unroll, unroll)
            picks = [index_ref.at[block, slot, pl.ds(first, unroll)] for slot in range(slots)]
            for u in range(unroll):
                point = base + first + u
                own = table[pl.ds(point * groups, groups), :]
                terms = []
                for slot in range(slots):
                    upwind = table[pl.ds(picks[slot][u], groups), :]
                    factor = inflow[slot, pl.ds(point, groups, stride=0), :]
                    terms.append(factor * (upwind - own))
                while len(terms) > 1:
                    terms = [a + b for a, b in zip(terms[::2], terms[1::2])]
                gathered[pl.ds((start + first + u) * groups, groups), :] = terms[0]

    @pl.loop(0, points // width)
    def _(part):
        several = width // LANES

        @pl.loop(0, several)
        def _(step):
            gather(part * several + step, pl.multiple_of(step * LANES, LANES))

        for group in range(groups):
            rows = slice(group * PAIR, (group + 1) * PAIR)
            speed = speed_rows[rows, :]
            for step in range(several):
                inner = slice(step * LANES, (step + 1) * LANES)
                outer = pl.ds(pl.multiple_of(part * width + step * LANES, LANES), LANES)
                picked = gathered[pl.ds(step * LANES * groups + group, LANES, stride=groups), :]
                advected = spec_ref[rows, outer] + speed * picked.T[:PAIR]
                result[part, rows, inner] = advected * gain_ref[rows, outer]
            copy_out(part, group).start()
        high, low = split2(result[part])
        both = dot(kernel_both[...], high)
        stokes = both[:depth] + both[depth:] + dot(kernel_both[:depth, :], low)
        half_parts = points // width // 2
        local = pl.ds(pl.multiple_of(lax.rem(part, half_parts) * width, width), width)
        kept = (part >= half_parts) == (odd == 1)

        @pl.when(kept)
        def _():
            keep_ref[:, local] = stokes

        @pl.when(jnp.logical_not(kept))
        def _():
            send_ref[:, local] = stokes

    @pl.loop(0, points // width)
    def _(part):
        for group in range(groups):
            copy_out(part, group).wait()


def advance(index, table, inflow, spectrum, gain, speed_rows, kernel_both, first, second):
    bins, points = spectrum.shape
    groups = bins // PAIR
    blocks = points // LANES
    half = jax.ShapeDtypeStruct((kernel_both.shape[0] // 2, points // 2), F32)
    return pl.pallas_call(
        functools.partial(advance_kernel, unroll=UNROLL),
        in_specs=[SMEM] + [VMEM] * 8,
        out_specs=[ANY, VMEM, VMEM, VMEM],
        out_shape=[jax.ShapeDtypeStruct((bins, points), F32), half, half, vmem(table.shape)],
        input_output_aliases={1: 3},
        scratch_shapes=[
            pltpu.VMEM((WIDTH * groups, LANES), F32),
            pltpu.VMEM((points // WIDTH, bins, WIDTH), F32),
            pltpu.SemaphoreType.DMA((points // WIDTH, groups)),
        ],
        compiler_params=params(12),
    )(index, table, inflow, spectrum, gain, speed_rows, kernel_both, first, second)


def regrid_kernel(slot_ref, high_ref, low_ref, stokes_ref, *refs, block_rows, own):
    out_ref = refs[-1]
    depth, points = stokes_ref.shape
    pairs = points // LANES
    odd = lax.axis_index("grp") % 2
    half = odd if own else 1 - odd
    if own:
        out_ref[...] = jnp.zeros(out_ref.shape, F32)
    lower = lax.broadcasted_iota(jnp.int32, (depth, LANES), 1) < block_rows
    for pair in range(pairs):
        part = stokes_ref[:, pair * LANES : (pair + 1) * LANES]
        both = jnp.concatenate([jnp.where(lower, part, 0.0), jnp.where(lower, 0.0, part)], 0)
        high, low = split2(both)
        place = half * pairs + pair
        rows = pl.ds(pl.multiple_of(place * LANES, LANES), LANES)
        terms = dot(high, high_ref[rows, :]) + dot(low, high_ref[rows, :]) + dot(high, low_ref[rows, :])
        for side in range(2):
            slot = slot_ref[2 * place + side]
            out_ref[slot] = out_ref[slot] + terms[side * depth : (side + 1) * depth]


def regrid(slots, mine, other, high, low, count, block_rows):
    total = []
    for stokes in (mine, other):
        total = [
            pl.pallas_call(
                functools.partial(regrid_kernel, block_rows=block_rows, own=not total),
                in_specs=[SMEM] + [VMEM] * (3 + len(total)),
                out_specs=VMEM,
                out_shape=jax.ShapeDtypeStruct((count, mine.shape[0], LANES), F32),
                input_output_aliases={4: 0} if total else {},
                compiler_params=params(4),
            )(slots, high, low, stokes, *total)
        ]
    return total[0]


def swap(value, axis, bit):
    count = lax.axis_size(axis)
    return lax.ppermute(value, axis, [(i, i ^ bit) for i in range(count)])


def sum_over(keep, send, axis):
    mine = keep + swap(send, axis, 1)
    bit = 2
    while bit < lax.axis_size(axis):
        mine = mine + swap(mine, axis, bit)
        bit *= 2
    return mine, swap(mine, axis, 1)


def exchange(value, even_bit, odd_bit):
    waves, groups = lax.axis_size("wave"), lax.axis_size("grp")
    pairs = [
        (w * groups + g, (w ^ (odd_bit if g % 2 else even_bit)) * groups + g)
        for w in range(waves)
        for g in range(groups)
    ]
    return lax.ppermute(value, ("wave", "grp"), pairs)


def scatter_sum(parts, bits, other_bits):
    for bit, other in zip(bits, other_bits):
        half = parts.shape[0] // 2
        parts = parts[:half] + exchange(parts[half:], bit, other)
    return parts[0]


def swap_halo(first, second):
    count = lax.axis_size("wave")
    first = swap(first, "wave", 1)
    inner = [(i, i + 1 if i % 2 else i - 1) for i in range(1, count - 1)]
    return first, lax.ppermute(second, "wave", inner)


def body(
    spectrum,
    edge_vectors,
    neighbours,
    halo_lists,
    group_speed,
    input_coef,
    dissipation,
    friction,
    wind_dir,
    drift_kernel,
    block_tile,
    block_weights,
):
    n_wave = lax.axis_size("wave")
    bins, points = spectrum.shape
    groups = bins // PAIR
    slots = neighbours.shape[0]
    rows = (points + 2 * halo_lists.shape[-1]) * groups
    bits = [1 << b for b in range(n_wave.bit_length() - 1)]
    other_bits = bits[1::-1] + bits[2:]
    spectrum, first, second = pick_halo(spectrum, halo_lists)
    first, second = swap_halo(first, second)
    index = neighbours.reshape(slots, points // LANES, LANES).transpose(1, 0, 2)
    edges = edge_vectors.reshape(2 * slots, points)
    table, inflow, gain, index, speed_rows, kernel_both, high, low, slot = prepare(
        spectrum,
        input_coef,
        dissipation,
        group_speed,
        edges,
        wind_dir,
        friction,
        drift_kernel,
        index,
        block_weights,
        block_tile,
        rows,
        (bits, other_bits),
    )
    updated, keep, send, _ = advance(
        index, table, inflow, spectrum, gain, speed_rows, kernel_both, first, second
    )
    mine, other = sum_over(keep, send, "grp")
    block_rows = block_weights.shape[1]
    parts = regrid(slot, mine, other, high, low, n_wave * TPW, block_rows)
    parts = parts.reshape(n_wave, TPW, *parts.shape[1:])
    drift = scatter_sum(parts, bits, other_bits)
    return updated, drift


def solution(mesh):
    in_specs = (
        P("grp", "wave"),
        P(None, None, "wave"),
        P(None, "wave"),
        P(None, "wave", None),
        P("grp"),
        P("grp"),
        P("grp"),
        P("wave"),
        P("wave"),
        P(None, "grp"),
        P("wave"),
        P("wave", None, None),
    )
    out_specs = (P("grp", "wave"), P("wave", None, "grp"))
    return jax.shard_map(body, mesh=mesh, in_specs=in_specs, out_specs=out_specs, check_vma=False)
```
